256 devices in a mesh: particle: 16 (over y, z_hi), coeffici: 8 (over x, core), half: 2 (over z_lo).
Axes of the slice: x: 4, y: 4, z: 8 (z_hi: 4, z_lo: 2; z = z_hi * 2 + z_lo), core: 2. Of those that a mesh axis runs over, the one named last changes fastest.
Arguments:
- residuals: float32 [2, 16384, 16384], P('half', 'particle', 'coeffici'), may hold values from -6 to 6
- loadings: float32 [2, 16384, 256], P('half', 'coeffici'), may hold values from -0.046875 to 0.046875
Outputs:
- new_loadings: float32 [2, 16384, 256], P('half', ('coeffici', 'particle'))
- rayleigh: float32 [2, 256, 256], P('half')
The draws below stay inside these ranges and needn't reach their ends.
All inputs are finite; a program needn't handle non-finite values.
Results may differ from the reference program's by a relative error of at most 0.00024.
Values sent between devices are 32-bit elements; how exact they have to be, the bound alone decides.
No kernel may reach another device: no remote copies, remote signals or barrier semaphores. Data moves between devices by JAX's collectives and lax.ppermute only.
A program may use at most 64 MiB of HBM per device.

```python
import jax
import jax.numpy as jnp
from jax import lax

C = 16384
K = 256
PARTICLES = 16384


def strengthened(result, key, source, target, blocks, factor):
    def block_of(axis_at):
        return (jnp.arange(result.shape[axis_at]) // (result.shape[axis_at] // blocks)).reshape((-1,) + (1,) * (result.ndim - 1 - axis_at))

    one_side = jax.random.permutation(key, blocks)[block_of(target)]
    far = (block_of(target) + blocks // 2) % blocks
    return jnp.where((block_of(source) == one_side) | (block_of(source) == far), factor * result, result)


def block_scale(stream_key, shape, split, least, high):
    def one(axis_at, blocks):
        heights = jax.random.uniform(jax.random.fold_in(jax.random.fold_in(stream_key, 6), axis_at), (blocks,), jnp.float32, least / len(split), high / len(split))
        return jnp.repeat(jnp.exp(heights), shape[axis_at] // blocks).reshape((-1,) + (1,) * (len(shape) - axis_at - 1))

    factor_of = one(*split[0])
    for cut in split[1:]:
        factor_of = factor_of * one(*cut)
    return factor_of


def gaussian(key, dims, deviation, limit, split=(), kind=jnp.bfloat16):
    drawn = jax.random.normal(key, dims, jnp.float32) * deviation
    if len(split) > 0:
        drawn = block_scale(key, dims, split, -0.22, 0.18) * drawn
    return jnp.clip(drawn, min=-limit, max=limit).astype(kind)


def bell_draw_with(rng, extent, scale, bound, split, heavy, held_as=jnp.bfloat16):
    values = scale * jax.random.normal(rng, extent, jnp.float32)
    if split:
        values = values * block_scale(rng, extent, split, -0.22, 0.18)
    return jnp.clip(strengthened(values, jax.random.fold_in(rng, 3), *heavy), -bound, bound).astype(held_as)


def setup_inputs(seed: int = 0) -> dict:
    splits = jax.random.split(jax.random.key(seed), 3)
    return {
        "residuals": bell_draw_with(splits[0], (2, PARTICLES, C), 1.0, 6.0, ((0, 2), (1, 16), (2, 8)), (1, 2, 16, 2.0), jnp.float32),
        "loadings": gaussian(splits[1], (2, C, K), C ** -0.5, 0.046875, ((0, 2), (1, 8)), jnp.float32),
    }


def reference(residuals, loadings):
    precise = lax.Precision.HIGHEST
    factor = PARTICLES ** -0.5
    covariances = []
    for half_idx in range(2):
        scores = jnp.dot(residuals[half_idx], loadings[half_idx], precision=precise, preferred_element_type=jnp.float32)
        covariance = jnp.dot(residuals[half_idx].T, scores, precision=precise, preferred_element_type=jnp.float32) * factor
        covariances.append(covariance)
    shrunk = []
    correlations = []
    for half_idx in range(2):
        covariance = covariances[half_idx]
        weighted = covariance * jax.nn.sigmoid(covariance * covariances[1 - half_idx])
        shrunk.append(weighted)
        correlations.append(jnp.dot(loadings[half_idx].T, weighted, precision=precise, preferred_element_type=jnp.float32) * factor)
    return jnp.stack(shrunk), jnp.stack(correlations)
```

```python
import functools

import jax
import jax.numpy as jnp
from jax import lax
from jax.experimental import pallas as pl
from jax.experimental.pallas import tpu as pltpu
from jax.sharding import PartitionSpec as P


F32 = jnp.float32
BF16 = jnp.bfloat16
VMEM = pl.BlockSpec(memory_space=pltpu.VMEM)
ANY = pl.BlockSpec(memory_space=pl.ANY)
LANE = 128

CORE, X1, X2 = 1, 2, 6
Y1, Y2, Z1, Z2 = 4, 12, 1, 3
PARTS = (
    (0, 88, (Y1, Y2, Z1, Z2)),
    (88, 88, (Y2, Y1, Z2, Z1)),
    (176, 40, (Z1, Z2, Y1, Y2)),
    (216, 40, (Z2, Z1, Y2, Y1)),
)


def mask_of(position, dims):
    mask = 0
    for place, dim in enumerate(dims):
        if position >> (len(dims) - 1 - place) & 1:
            mask ^= dim
    return mask


def swap(value, axis, mask):
    return lax.ppermute(value, axis, [(s, s ^ mask) for s in range(lax.axis_size(axis))])


def parts_of(value):
    high = value.astype(BF16)
    return high, (value - high.astype(F32)).astype(BF16)


def dot(left, right, dims=(((1,), (0,)), ((), ()))):
    return lax.dot_general(left, right, dims, preferred_element_type=F32)


def dot3(lh, ll, rh, rl):
    return dot(lh, rh) + dot(ll, rh) + dot(lh, rl)


def params(mib):
    return pltpu.CompilerParams(vmem_limit_bytes=mib << 20)


def shape(*dims, dtype=F32):
    return jax.ShapeDtypeStruct(dims, dtype)


def scores_kernel(first, core, res, load, *refs):
    if first:
        p_out, q_out, lh, ll, buf, lbuf, sems = refs
        p_out, q_out = p_out, q_out
    else:
        low, p_out, q_out, buf, sems = refs
        lh, ll = load, low
    me = lax.axis_index("coeffici")
    rows = p_out.shape[1]
    copies = []
    if first:
        fetch = pltpu.make_async_copy(load, lbuf, sems.at[4])
        fetch.start()
    for step in range(4):
        block = me ^ mask_of(step, (X1, X2)) ^ core
        copy = pltpu.make_async_copy(
            res.at[pl.ds(pl.multiple_of(block * rows, rows), rows)], buf.at[step], sems.at[step]
        )
        copy.start()
        copies.append(copy)
    if first:
        fetch.wait()
        lh[...], ll[...] = parts_of(lbuf[...])
    for step in range(4):
        copies[step].wait()
        high, low_part = parts_of(buf[step])
        out = dot3(high, low_part, lh[...], ll[...])
        p_out[step] = out[:, :LANE]
        q_out[(step >> 1) | ((step & 1) << 1)] = out[:, LANE:]


def scores_far(res, load):
    rows, coefs = res.shape
    block = rows // 8
    k = load.shape[1]
    return pl.pallas_call(
        functools.partial(scores_kernel, True, CORE),
        out_shape=(
            shape(4, block, LANE),
            shape(4, block, LANE),
            shape(coefs, k, dtype=BF16),
            shape(coefs, k, dtype=BF16),
        ),
        in_specs=[ANY, ANY],
        out_specs=(VMEM,) * 4,
        scratch_shapes=[
            pltpu.VMEM((4, block, coefs), F32),
            pltpu.VMEM((coefs, k), F32),
            pltpu.SemaphoreType.DMA((5,)),
        ],
        compiler_params=params(20),
        cost_estimate=pl.CostEstimate(flops=3 * rows * coefs * k, bytes_accessed=6 << 20, transcendentals=0),
        name="scores_far",
    )(res, load)


def scores_near(res, lh, ll):
    rows, coefs = res.shape
    block = rows // 8
    k = lh.shape[1]
    return pl.pallas_call(
        functools.partial(scores_kernel, False, 0),
        out_shape=(shape(4, block, LANE), shape(4, block, LANE)),
        in_specs=[ANY, VMEM, VMEM],
        out_specs=(VMEM,) * 2,
        scratch_shapes=[pltpu.VMEM((4, block, coefs), F32), pltpu.SemaphoreType.DMA((4,))],
        compiler_params=params(20),
        cost_estimate=pl.CostEstimate(flops=3 * rows * coefs * k, bytes_accessed=6 << 20, transcendentals=0),
        name="scores_near",
    )(res, lh, ll)


def own_kernel(*refs):
    p, q = refs[8], refs[9]
    for out, (a, b, c, d) in ((p, refs[0:4]), (q, refs[4:8])):
        out[...] = (a[0] + b[0] + c[0] + d[...]).T


def own_block(p, q):
    rows = p[0].shape[1]
    return pl.pallas_call(
        own_kernel,
        out_shape=(shape(LANE, rows), shape(LANE, rows)),
        in_specs=[VMEM] * 8,
        out_specs=(VMEM,) * 2,
        compiler_params=params(8),
        cost_estimate=pl.CostEstimate(flops=1 << 18, bytes_accessed=1 << 20, transcendentals=0),
        name="own_block",
    )(*p, *q)


def covariance_kernel(res, *refs):
    pieces, outs = refs[:16], refs[16 : 16 + len(PARTS)]
    sh, sl, buf, sems = refs[16 + len(PARTS) :]
    coeffici = lax.axis_index("coeffici")
    particle = lax.axis_index("particle")
    dims = PARTS[0][2]
    copies = []
    for at in range(16):
        block = particle ^ mask_of(15 - at, dims)
        copy = pltpu.make_async_copy(
            res.at[:, pl.ds(pl.multiple_of(block * LANE, LANE), LANE)],
            buf.at[at // 2, :, pl.ds(at % 2 * LANE, LANE)],
            sems.at[at],
        )
        copy.start()
        copies.append(copy)
    for at in range(8):
        block = coeffici ^ mask_of(at, (CORE, X1, X2))
        where = pl.ds(pl.multiple_of(block * LANE, LANE), LANE)
        for side in range(2):
            high, low = parts_of(pieces[2 * at + side][...])
            rows = pl.ds(side * LANE, LANE)
            sh[rows, where] = high
            sl[rows, where] = low
    for pair in range(8):
        copies[2 * pair].wait()
        copies[2 * pair + 1].wait()
        rh, rl = parts_of(buf[pair])
        out = dot3(sh[...], sl[...], rh, rl)
        for side in range(2):
            mask = mask_of(15 - (2 * pair + side), dims)
            for ref, (start, size, order) in zip(outs, PARTS):
                place = [p for p in range(16) if mask_of(p, order) == mask][0]
                ref[place] = out[start : start + size, side * LANE : (side + 1) * LANE]


def covariance(res, pieces):
    rows, coefs = res.shape
    return pl.pallas_call(
        covariance_kernel,
        out_shape=tuple(shape(16, size, LANE) for _, size, _ in PARTS),
        in_specs=[ANY] + [VMEM] * 16,
        out_specs=(VMEM,) * len(PARTS),
        scratch_shapes=[
            pltpu.VMEM((2 * LANE, rows), BF16),
            pltpu.VMEM((2 * LANE, rows), BF16),
            pltpu.VMEM((8, rows, 2 * LANE), F32),
            pltpu.SemaphoreType.DMA((16,)),
        ],
        compiler_params=params(24),
        cost_estimate=pl.CostEstimate(flops=6 * rows * coefs * 2 * LANE, bytes_accessed=12 << 20, transcendentals=0),
        name="covariance",
    )(res, *pieces)


def shrink_kernel(factor, load, *refs):
    n = len(PARTS)
    mine, other = refs[:n], refs[n : 2 * n]
    w_out, corr_out, lbuf, cbuf, sem = refs[2 * n :]
    particle = lax.axis_index("particle")
    coeffici = lax.axis_index("coeffici")
    copy = pltpu.make_async_copy(
        load.at[pl.ds(pl.multiple_of(particle * LANE, LANE), LANE)], lbuf, sem
    )
    copy.start()
    cov = jnp.concatenate([r[...] for r in mine], axis=0) * factor
    far = jnp.concatenate([r[...] for r in other], axis=0) * factor
    weighted = (cov * jax.nn.sigmoid(cov * far)).T
    w_out[...] = weighted
    copy.wait()
    lh, ll = parts_of(lbuf[...].T)
    wh, wl = parts_of(weighted)
    cbuf[...] = dot3(lh, ll, wh, wl) * factor
    size = cbuf.shape[0] // 8
    for at in range(8):
        block = coeffici ^ mask_of(at, (CORE, X1, X2))
        corr_out[at] = cbuf[pl.ds(pl.multiple_of(block * size, size), size)]


def shrink(factor, load, mine, other):
    k = load.shape[1]
    return pl.pallas_call(
        functools.partial(shrink_kernel, factor),
        out_shape=(shape(LANE, k), shape(8, k // 8, k)),
        in_specs=[ANY] + [VMEM] * (2 * len(mine)),
        out_specs=(VMEM,) * 2,
        scratch_shapes=[pltpu.VMEM((LANE, k), F32), pltpu.VMEM((k, k), F32), pltpu.SemaphoreType.DMA],
        compiler_params=params(8),
        cost_estimate=pl.CostEstimate(flops=6 * LANE * k * k, bytes_accessed=1 << 20, transcendentals=LANE * k),
        name="shrink",
    )(load, *mine, *other)


def assemble_kernel(*refs):
    pieces, out = refs[:8], refs[8]
    coeffici = lax.axis_index("coeffici")
    size = out.shape[0] // 8
    for at in range(8):
        block = coeffici ^ mask_of(at, (CORE, X1, X2))
        out[pl.ds(pl.multiple_of(block * size, size), size)] = pieces[at][...]


def assemble(pieces):
    size, k = pieces[0].shape
    return pl.pallas_call(
        assemble_kernel,
        out_shape=shape(8 * size, k),
        in_specs=[VMEM] * 8,
        out_specs=VMEM,
        compiler_params=params(4),
        name="assemble",
    )(*pieces)


def reduce_half(value, axis, dims):
    terms = [value]
    for dim in dims:
        half = terms[0].shape[0] // 2
        send = functools.reduce(jnp.add, [t[half : 2 * half] for t in terms])
        terms = [t[:half] for t in terms] + [swap(send, axis, dim)]
    return terms


def local(residuals, loadings):
    res, load = residuals[0], loadings[0]
    factor = (res.shape[0] * lax.axis_size("particle")) ** -0.5

    far_p, far_q, lh, ll = scores_far(res, load)
    got_p, got_q = swap(far_p, "coeffici", CORE), swap(far_q, "coeffici", CORE)
    near_p, near_q = scores_near(res, lh, ll)

    def partial_sums(near, got, first, second):
        send = near[2:] + got[2:]
        one = swap(send, "coeffici", first)
        send = near[1] + got[1] + one[1]
        two = swap(send, "coeffici", second)
        return near, got, one, two

    p = partial_sums(near_p, got_p, X1, X2)
    q = partial_sums(near_q, got_q, X2, X1)
    own_p, own_q = own_block(p, q)

    def gathered(own, first, second):
        a = swap(own, "coeffici", first)
        b = swap(own, "coeffici", second)
        c = swap(a, "coeffici", second)
        far = [swap(v, "coeffici", CORE) for v in (own, a, b, c)]
        return [own, a, b, c], far

    gp, gp_far = gathered(own_p, X1, X2)
    gq, gq_far = gathered(own_q, X2, X1)
    pieces = []
    for ps, qs in ((gp, gq), (gp_far, gq_far)):
        for at_p, at_q in ((0, 0), (2, 1), (1, 2), (3, 3)):
            pieces += [ps[at_p], qs[at_q]]

    sums = covariance(res, pieces)
    mine = []
    for value, (_, _, order) in zip(sums, PARTS):
        mine.append(functools.reduce(jnp.add, [t[0] for t in reduce_half(value, "particle", order)]))
    other = [swap(v, "half", 1) for v in mine]
    weighted, corr = shrink(factor, load, mine, other)

    one = swap(corr[4:], "coeffici", CORE)
    corr = corr[:4] + one
    parts = [corr[0]] + [swap(corr[at], "coeffici", mask_of(at, (X1, X2))) for at in (1, 2, 3)]
    total = (parts[0] + parts[1]) + (parts[2] + parts[3])
    for dims in ((Y1, Y2), (Z1, Z2)):
        a, b, c = (swap(total, "particle", m) for m in (dims[1], dims[0], dims[0] ^ dims[1]))
        total = (total + a) + (b + c)
    blocks = [total] + [swap(total, "coeffici", mask_of(at, (X1, X2))) for at in (1, 2, 3)]
    blocks += [swap(b, "coeffici", CORE) for b in blocks]
    return weighted[None], assemble(blocks)[None]


def solution(mesh):
    in_specs = (P("half", "particle", "coeffici"), P("half", "coeffici", None))
    out_specs = (P("half", ("coeffici", "particle"), None), P("half", None, None))
    return jax.shard_map(local, mesh=mesh, in_specs=in_specs, out_specs=out_specs, check_vma=False)
```

```python
import functools

import jax
import jax.numpy as jnp
from jax import lax
from jax.experimental import pallas as pl
from jax.experimental.pallas import tpu as pltpu
from jax.sharding import PartitionSpec as P


F32 = jnp.float32
BF16 = jnp.bfloat16
VMEM = pl.BlockSpec(memory_space=pltpu.VMEM)
HBM = pl.BlockSpec(memory_space=pltpu.HBM)
LANE = 128

CORE, X1, X2 = 1, 2, 6
Y1, Y2, Z1, Z2 = 4, 12, 1, 3
RING = (0, 1, 3, 2)
ORDERS = ((Y1, Y2, Z1, Z2), (Y2, Y1, Z2, Z1))


def swap(value, axis, mask):
    return lax.ppermute(value, axis, [(s, s ^ mask) for s in range(lax.axis_size(axis))])


def split(value):
    high = value.astype(BF16)
    return high, (value - high.astype(F32)).astype(BF16)


def dot(left, right):
    return lax.dot_general(left, right, (((1,), (0,)), ((), ())), preferred_element_type=F32)


def dot3(lh, ll, rh, rl):
    return dot(lh, rh) + dot(ll, rh) + dot(lh, rl)


def at(index, size):
    return pl.ds(pl.multiple_of(index * size, size), size)


def params(mib):
    return pltpu.CompilerParams(vmem_limit_bytes=mib << 20)


def shape(*dims, dtype=F32):
    return jax.ShapeDtypeStruct(dims, dtype)


def cost(flops, mib):
    return pl.CostEstimate(flops=flops, bytes_accessed=mib << 20, transcendentals=0)


def scores_kernel(chunks, res, load, near, far, rbuf, lbuf, acc, sems):
    me = lax.axis_index("coeffici")
    depth = lbuf.shape[1]

    def copies(step):
        return (
            pltpu.make_async_copy(res.at[:, at(step, depth)], rbuf.at[step], sems.at[0, step]),
            pltpu.make_async_copy(load.at[at(step, depth)], lbuf.at[step], sems.at[1, step]),
        )

    for step in range(chunks):
        for copy in copies(step):
            copy.start()
    acc[...] = jnp.zeros_like(acc)
    rows = acc.shape[0] // 2

    @pl.loop(0, chunks)
    def _(step):
        for copy in copies(step):
            copy.wait()
        lh, ll = split(lbuf[step])

        @pl.loop(0, 2)
        def _(half):
            where = at(half, rows)
            high, low = split(rbuf[step, where])
            acc[where] += dot3(high, low, lh, ll)

    size = near.shape[2]

    @pl.loop(0, 8)
    def _(block):
        mask = me ^ block
        second = mask >> 2
        first = ((mask >> 1) & 1) ^ second
        where = at(block, size)
        for out, core in ((near, 0), (far, 1)):

            @pl.when((mask & 1) == core)
            def _():
                out[0, 2 * first + second] = acc[where, :LANE]
                out[1, 2 * second + first] = acc[where, LANE:]


def scores(res, load):
    rows, coefs = res.shape
    k = load.shape[1]
    chunks = 4
    out = shape(2, 4, rows // 8, LANE)
    return pl.pallas_call(
        functools.partial(scores_kernel, chunks),
        out_shape=(out, out),
        in_specs=[HBM, HBM],
        out_specs=(VMEM, VMEM),
        scratch_shapes=[
            pltpu.VMEM((chunks, rows, coefs // chunks), F32),
            pltpu.VMEM((chunks, coefs // chunks, k), F32),
            pltpu.VMEM((rows, k), F32),
            pltpu.SemaphoreType.DMA((2, chunks)),
        ],
        compiler_params=params(24),
        cost_estimate=cost(6 * rows * coefs * k, 10),
        name="scores",
    )(res, load)


def own_kernel(near, got, p1, p2, q1, q2, p, q):
    p[...] = (near[0, 0] + got[0, 0] + p1[0] + p2[...]).T
    q[...] = (near[1, 0] + got[1, 0] + q1[0] + q2[...]).T


def own_block(near, got, p1, p2, q1, q2):
    rows = near.shape[2]
    return pl.pallas_call(
        own_kernel,
        out_shape=(shape(LANE, rows), shape(LANE, rows)),
        in_specs=[VMEM] * 6,
        out_specs=(VMEM, VMEM),
        compiler_params=params(4),
        cost_estimate=cost(1 << 18, 1),
        name="own_block",
    )(near, got, p1, p2, q1, q2)


def covariance_part(part, res, st, out):
    particle = lax.axis_index("particle")
    y, z = particle >> 2, particle & 3
    size = out.shape[1]

    @pl.loop(0, 4)
    def _(zp):
        high_bit, low_bit = zp >> 1, zp & 1
        zm = (high_bit ^ (3 * low_bit)) if part == 0 else ((3 * high_bit) ^ low_bit)
        halves = [res[:, at(4 * (2 * part + n) + (z ^ zm), LANE)] for n in range(2)]
        rh, rl = split(jnp.concatenate(halves, axis=1))
        both = dot(st[...], rh)
        k = both.shape[0] // 2
        cov = both[:k] + both[k:] + dot(st[:k], rl)
        for block in range(4):
            mask = y ^ block
            second = mask >> 1
            first = (mask & 1) ^ second
            place = (2 * first + second) if part == 0 else (2 * second + first)
            out[4 * place + zp] = cov[size * block : size * (block + 1)]


def first_kernel(res, own_p, own_q, a_p, a_q, b_p, b_q, c1, c2, st, out):
    me = lax.axis_index("coeffici")

    def put(mask, p, q):
        where = at(me ^ mask, LANE)
        for n, piece in enumerate((p, q)):
            high, low = split(piece)
            st[n * LANE : (n + 1) * LANE, where] = high
            st[(n + 2) * LANE : (n + 3) * LANE, where] = low

    put(0, own_p[...], own_q[...])
    put(X1, b_p[0], a_q[...])
    put(X2, a_p[...], b_q[0])
    put(X1 ^ X2, b_p[1], b_q[1])
    put(CORE, c1[0], c1[2])
    put(CORE ^ X1, c2[0], c1[3])
    put(CORE ^ X2, c1[1], c2[2])
    put(CORE ^ X1 ^ X2, c2[1], c2[3])
    covariance_part(0, res, st, out)


def second_kernel(res, st, out):
    covariance_part(1, res, st, out)


def covariance_first(res, *pieces):
    rows, coefs = res.shape
    return pl.pallas_call(
        first_kernel,
        out_shape=(shape(4 * LANE, rows, dtype=BF16), shape(16, 64, 2 * LANE)),
        in_specs=[VMEM] * (1 + len(pieces)),
        out_specs=(VMEM, VMEM),
        compiler_params=params(24),
        cost_estimate=cost(3 * rows * coefs * 2 * LANE, 4),
        name="covariance_first",
    )(res, *pieces)


def covariance_second(res, st):
    rows, coefs = res.shape
    return pl.pallas_call(
        second_kernel,
        out_shape=shape(16, 64, 2 * LANE),
        in_specs=[VMEM, VMEM],
        out_specs=VMEM,
        compiler_params=params(24),
        cost_estimate=cost(3 * rows * coefs * 2 * LANE, 4),
        name="covariance_second",
    )(res, st)


def shrink_kernel(factor, load, mine, other, w_out, corr_out, cbuf):
    particle = lax.axis_index("particle")
    y, z = particle >> 2, particle & 3
    core = lax.axis_index("coeffici") & 1
    corr = None
    for n in range(4):
        cols = slice((n & 1) * LANE, (n & 1) * LANE + LANE)
        cov = mine[n >> 1, :, cols] * factor
        far = other[n >> 1, :, cols] * factor
        weighted = cov * jax.nn.sigmoid(cov * far)
        mask = y ^ n
        w_out[mask ^ (mask >> 1)] = weighted
        wh, wl = split(weighted)
        lh, ll = split(load[at(4 * n + z, LANE)])
        term = dot3(wh, wl, lh, ll)
        corr = term if corr is None else corr + term
    cbuf[...] = corr * factor
    for n in range(2):
        rows = cbuf[at(core ^ n, 32)]
        corr_out[n, :32] = rows[:, :LANE]
        corr_out[n, 32:] = rows[:, LANE:]


def shrink(factor, load, mine, other):
    return pl.pallas_call(
        functools.partial(shrink_kernel, factor),
        out_shape=(shape(4, 64, LANE), shape(2, 64, LANE)),
        in_specs=[VMEM] * 3,
        out_specs=(VMEM, VMEM),
        scratch_shapes=[pltpu.VMEM((64, 2 * LANE), F32)],
        compiler_params=params(8),
        cost_estimate=cost(6 * 64 * 512 * 256, 1),
        name="shrink",
    )(load, mine, other)


def assemble_kernel(w, corr, r1, r2, r3, far0, far, w_out, corr_out, wbuf, cbuf):
    y = lax.axis_index("particle") >> 2
    core = lax.axis_index("coeffici") & 1
    got = (None, r1, r2, r3)
    for n in range(4):
        block = y ^ RING[n]
        wbuf[at(block, 64)] = w[0] if n == 0 else got[n][1]
        for c in range(2):
            if n == 0:
                piece = (corr if c == 0 else far0)[...]
            else:
                piece = got[n][0] if c == 0 else far[n - 1]
            where = at(2 * block + (core ^ c), 32)
            cbuf[where, :LANE] = piece[:32]
            cbuf[where, LANE:] = piece[32:]
    w_out[...] = wbuf[...].T
    corr_out[...] = cbuf[...].T


def assemble(*args):
    k = 2 * LANE
    return pl.pallas_call(
        assemble_kernel,
        out_shape=(shape(LANE, k), shape(k, k)),
        in_specs=[VMEM] * len(args),
        out_specs=(VMEM, VMEM),
        scratch_shapes=[pltpu.VMEM((k, LANE), F32), pltpu.VMEM((k, k), F32)],
        compiler_params=params(4),
        name="assemble",
    )(*args)


def reduce_half(value, dims):
    terms = [value]
    for dim in dims:
        half = terms[0].shape[0] // 2
        send = functools.reduce(jnp.add, [t[half : 2 * half] for t in terms])
        terms = [t[:half] for t in terms] + [swap(send, "particle", dim)]
    return functools.reduce(jnp.add, [t[0] for t in terms])


def ring_sum(value, axis, first, second):
    a, b, c = (swap(value, axis, m) for m in (first, second, first ^ second))
    return (value + a) + (b + c)


def local(residuals, loadings):
    res, load = residuals[0], loadings[0]
    factor = (res.shape[0] * lax.axis_size("particle")) ** -0.5

    near, far = scores(res, load)
    got = swap(far, "coeffici", CORE)

    p1 = swap(near[0, 2:] + got[0, 2:], "coeffici", X1)
    q1 = swap(near[1, 2:] + got[1, 2:], "coeffici", X2)
    p2 = swap(near[0, 1] + got[0, 1] + p1[1], "coeffici", X2)
    q2 = swap(near[1, 1] + got[1, 1] + q1[1], "coeffici", X1)
    own_p, own_q = own_block(near, got, p1, p2, q1, q2)

    a_p, a_q = swap(own_p, "coeffici", X2), swap(own_q, "coeffici", X1)
    c1 = swap(jnp.stack([own_p, a_p, own_q, a_q]), "coeffici", CORE)
    b_p = swap(jnp.stack([own_p, a_p]), "coeffici", X1)
    b_q = swap(jnp.stack([own_q, a_q]), "coeffici", X2)
    c2 = swap(jnp.concatenate([b_p, b_q]), "coeffici", CORE)

    st, part_p = covariance_first(res, own_p, own_q, a_p, a_q, b_p, b_q, c1, c2)
    part_q = covariance_second(res, st)
    mine = jnp.stack([reduce_half(v, order) for v, order in zip((part_p, part_q), ORDERS)])
    other = swap(mine, "half", 1)
    w, corr = shrink(factor, load, mine, other)

    corr = corr[0] + swap(corr[1], "coeffici", CORE)
    corr = ring_sum(corr, "coeffici", X1, X2)
    corr = ring_sum(corr, "particle", Z1, Z2)
    far0 = swap(corr, "coeffici", CORE)
    got = [swap(jnp.stack([corr, w[n]]), "particle", m) for n, m in ((1, Y1), (2, Y2), (3, Y1 ^ Y2))]
    far = swap(jnp.stack([g[0] for g in got]), "coeffici", CORE)
    weighted, rayleigh = assemble(w, corr, *got, far0, far)
    return weighted[None], rayleigh[None]


def solution(mesh):
    in_specs = (P("half", "particle", "coeffici"), P("half", "coeffici", None))
    out_specs = (P("half", ("coeffici", "particle"), None), P("half", None, None))
    return jax.shard_map(local, mesh=mesh, in_specs=in_specs, out_specs=out_specs, check_vma=False)
```

```python
import functools

import jax
import jax.numpy as jnp
from jax import lax
from jax.experimental import pallas as pl
from jax.experimental.pallas import tpu as pltpu
from jax.sharding import PartitionSpec as P


F32 = jnp.float32
BF16 = jnp.bfloat16
VMEM = pl.BlockSpec(memory_space=pltpu.VMEM)
HBM = pl.BlockSpec(memory_space=pltpu.HBM)
LANE = 128

CORE, X1, X2 = 1, 2, 6
Y1, Y2, Z1, Z2 = 4, 12, 1, 3
RING = (0, 1, 3, 2)
ORDERS = ((Y1, Y2, Z1, Z2), (Y2, Y1, Z2, Z1))


def swap(value, axis, mask):
    return lax.ppermute(value, axis, [(s, s ^ mask) for s in range(lax.axis_size(axis))])


def split(value):
    high = value.astype(BF16)
    return high, (value - high.astype(F32)).astype(BF16)


def dot(left, right):
    return lax.dot_general(left, right, (((1,), (0,)), ((), ())), preferred_element_type=F32)


def dot3(lh, ll, rh, rl):
    return dot(lh, rh) + dot(ll, rh) + dot(lh, rl)


def at(index, size):
    return pl.ds(pl.multiple_of(index * size, size), size)


def params(mib):
    return pltpu.CompilerParams(vmem_limit_bytes=mib << 20)


def shape(*dims, dtype=F32):
    return jax.ShapeDtypeStruct(dims, dtype)


def cost(flops, mib):
    return pl.CostEstimate(flops=flops, bytes_accessed=mib << 20, transcendentals=0)


def product(side, rows_of, lh_of, acc, out):
    me = lax.axis_index("coeffici")
    size = out.shape[2]
    for step in range(4):
        lh, ll = lh_of(step)
        high, low = split(rows_of(step))
        term = dot3(high, low, lh, ll)
        if step == 0:
            acc[...] = term
        else:
            acc[...] += term
    for t in range(4):
        mask = me ^ (2 * t + ((me & 1) ^ side))
        second = mask >> 2
        first = ((mask >> 1) & 1) ^ second
        rows = slice(t * size, (t + 1) * size)
        out[0, 2 * first + second] = acc[rows, :LANE]
        out[1, 2 * second + first] = acc[rows, LANE:]


def blocks_of(side, ref, size, cols):
    core = lax.axis_index("coeffici") & 1
    return jnp.concatenate([ref[at(2 * t + (core ^ side), size), cols] for t in range(4)])


def far_kernel(res, load, far, rbuf, lbuf, lh, ll, acc, fsems, lsems, nsems):
    core = lax.axis_index("coeffici") & 1
    size, depth = far.shape[2], lbuf.shape[0] // 4
    copies, later = [], []
    for step in range(4):
        cols = slice(step * depth, (step + 1) * depth)
        some = [pltpu.make_async_copy(load.at[cols], lbuf.at[cols], lsems.at[step])]
        for t in range(4):
            rows = at(2 * t + (core ^ 1), size)
            some.append(pltpu.make_async_copy(res.at[rows, cols], rbuf.at[rows, cols], fsems.at[step, t]))
        for copy in some:
            copy.start()
        copies.append(some)
    for t in range(4):
        rows = at(2 * t + core, size)
        later.append(pltpu.make_async_copy(res.at[rows], rbuf.at[rows], nsems.at[t]))
        later[-1].start()

    def loading(step):
        for copy in copies[step]:
            copy.wait()
        cols = slice(step * depth, (step + 1) * depth)
        high, low = split(lbuf[cols])
        lh[cols], ll[cols] = high, low
        return high, low

    def rows_of(step):
        return blocks_of(1, rbuf, size, slice(step * depth, (step + 1) * depth))

    product(1, rows_of, loading, acc, far)
    for copy in later:
        copy.wait()


def near_kernel(rbuf, lh, ll, near, acc):
    size, depth = near.shape[2], lh.shape[0] // 4

    def loading(step):
        cols = slice(step * depth, (step + 1) * depth)
        return lh[cols], ll[cols]

    def rows_of(step):
        return blocks_of(0, rbuf, size, slice(step * depth, (step + 1) * depth))

    product(0, rows_of, loading, acc, near)


def scores_far(res, load):
    rows, coefs = res.shape
    k = load.shape[1]
    return pl.pallas_call(
        far_kernel,
        out_shape=(
            shape(2, 4, rows // 8, LANE),
            shape(rows, coefs),
            shape(coefs, k),
            shape(coefs, k, dtype=BF16),
            shape(coefs, k, dtype=BF16),
        ),
        in_specs=[HBM, HBM],
        out_specs=(VMEM,) * 5,
        scratch_shapes=[
            pltpu.VMEM((rows // 2, k), F32),
            pltpu.SemaphoreType.DMA((4, 4)),
            pltpu.SemaphoreType.DMA((4,)),
            pltpu.SemaphoreType.DMA((4,)),
        ],
        compiler_params=params(16),
        cost_estimate=cost(3 * rows * coefs * k, 10),
        name="scores_far",
    )(res, load)


def scores_near(res, lh, ll):
    rows, coefs = res.shape
    k = lh.shape[1]
    return pl.pallas_call(
        near_kernel,
        out_shape=shape(2, 4, rows // 8, LANE),
        in_specs=[VMEM] * 3,
        out_specs=VMEM,
        scratch_shapes=[pltpu.VMEM((rows // 2, k), F32)],
        compiler_params=params(24),
        cost_estimate=cost(3 * rows * coefs * k, 10),
        name="scores_near",
    )(res, lh, ll)


def own_kernel(near, got, p1, p2, q1, q2, p, q):
    p[...] = (near[0, 0] + got[0, 0] + p1[0] + p2[...]).T
    q[...] = (near[1, 0] + got[1, 0] + q1[0] + q2[...]).T


def own_block(near, got, p1, p2, q1, q2):
    rows = near.shape[2]
    return pl.pallas_call(
        own_kernel,
        out_shape=(shape(LANE, rows), shape(LANE, rows)),
        in_specs=[VMEM] * 6,
        out_specs=(VMEM, VMEM),
        compiler_params=params(4),
        cost_estimate=cost(1 << 18, 1),
        name="own_block",
    )(near, got, p1, p2, q1, q2)


def covariance_part(part, res, st, out):
    particle = lax.axis_index("particle")
    y, z = particle >> 2, particle & 3
    size = out.shape[1]

    @pl.loop(0, 4)
    def _(zp):
        high_bit, low_bit = zp >> 1, zp & 1
        zm = (high_bit ^ (3 * low_bit)) if part == 0 else ((3 * high_bit) ^ low_bit)
        halves = [res[:, at(4 * (2 * part + n) + (z ^ zm), LANE)] for n in range(2)]
        rh, rl = split(jnp.concatenate(halves, axis=1))
        both = dot(st[...], rh)
        k = both.shape[0] // 2
        cov = both[:k] + both[k:] + dot(st[:k], rl)
        for block in range(4):
            mask = y ^ block
            second = mask >> 1
            first = (mask & 1) ^ second
            place = (2 * first + second) if part == 0 else (2 * second + first)
            out[4 * place + zp] = cov[size * block : size * (block + 1)]


def first_kernel(res, own_p, own_q, a_p, a_q, b_p, b_q, far, st, out):
    me = lax.axis_index("coeffici")

    def put(mask, p, q):
        where = at(me ^ mask, LANE)
        for n, piece in enumerate((p, q)):
            high, low = split(piece)
            st[n * LANE : (n + 1) * LANE, where] = high
            st[(n + 2) * LANE : (n + 3) * LANE, where] = low

    put(0, own_p[...], own_q[...])
    put(X1, b_p[0], a_q[...])
    put(X2, a_p[...], b_q[0])
    put(X1 ^ X2, b_p[1], b_q[1])
    put(CORE, far[0], far[2])
    put(CORE ^ X1, far[4], far[3])
    put(CORE ^ X2, far[1], far[6])
    put(CORE ^ X1 ^ X2, far[5], far[7])
    covariance_part(0, res, st, out)


def second_kernel(res, st, out):
    covariance_part(1, res, st, out)


def covariance_first(res, *pieces):
    rows, coefs = res.shape
    return pl.pallas_call(
        first_kernel,
        out_shape=(shape(4 * LANE, rows, dtype=BF16), shape(16, 64, 2 * LANE)),
        in_specs=[VMEM] * (1 + len(pieces)),
        out_specs=(VMEM, VMEM),
        compiler_params=params(24),
        cost_estimate=cost(3 * rows * coefs * 2 * LANE, 4),
        name="covariance_first",
    )(res, *pieces)


def covariance_second(res, st):
    rows, coefs = res.shape
    return pl.pallas_call(
        second_kernel,
        out_shape=shape(16, 64, 2 * LANE),
        in_specs=[VMEM, VMEM],
        out_specs=VMEM,
        compiler_params=params(24),
        cost_estimate=cost(3 * rows * coefs * 2 * LANE, 4),
        name="covariance_second",
    )(res, st)


def shrink_kernel(factor, load, mine, other, w_out, corr_out, cbuf):
    particle = lax.axis_index("particle")
    y, z = particle >> 2, particle & 3
    core = lax.axis_index("coeffici") & 1
    corr = None
    for n in range(4):
        cols = slice((n & 1) * LANE, (n & 1) * LANE + LANE)
        cov = mine[n >> 1, :, cols] * factor
        far = other[n >> 1, :, cols] * factor
        weighted = cov * jax.nn.sigmoid(cov * far)
        mask = y ^ n
        w_out[mask ^ (mask >> 1)] = weighted
        wh, wl = split(weighted)
        lh, ll = split(load[at(4 * n + z, LANE)])
        term = dot3(wh, wl, lh, ll)
        corr = term if corr is None else corr + term
    cbuf[...] = corr * factor
    for n in range(2):
        rows = cbuf[at(core ^ n, 32)]
        corr_out[n, :32] = rows[:, :LANE]
        corr_out[n, 32:] = rows[:, LANE:]


def shrink(factor, load, mine, other):
    return pl.pallas_call(
        functools.partial(shrink_kernel, factor),
        out_shape=(shape(4, 64, LANE), shape(2, 64, LANE)),
        in_specs=[VMEM] * 3,
        out_specs=(VMEM, VMEM),
        scratch_shapes=[pltpu.VMEM((64, 2 * LANE), F32)],
        compiler_params=params(8),
        cost_estimate=cost(6 * 64 * 512 * 256, 1),
        name="shrink",
    )(load, mine, other)


def assemble_kernel(w, corr, r1, r2, r3, far0, far, w_out, corr_out, wbuf, cbuf):
    y = lax.axis_index("particle") >> 2
    core = lax.axis_index("coeffici") & 1
    got = (None, r1, r2, r3)
    for n in range(4):
        block = y ^ RING[n]
        wbuf[at(block, 64)] = w[0] if n == 0 else got[n][1]
        for c in range(2):
            if n == 0:
                piece = (corr if c == 0 else far0)[...]
            else:
                piece = got[n][0] if c == 0 else far[n - 1]
            where = at(2 * block + (core ^ c), 32)
            cbuf[where, :LANE] = piece[:32]
            cbuf[where, LANE:] = piece[32:]
    w_out[...] = wbuf[...].T
    corr_out[...] = cbuf[...].T


def assemble(*args):
    k = 2 * LANE
    return pl.pallas_call(
        assemble_kernel,
        out_shape=(shape(LANE, k), shape(k, k)),
        in_specs=[VMEM] * len(args),
        out_specs=(VMEM, VMEM),
        scratch_shapes=[pltpu.VMEM((k, LANE), F32), pltpu.VMEM((k, k), F32)],
        compiler_params=params(4),
        name="assemble",
    )(*args)


def reduce_half(value, dims):
    terms = [value]
    for dim in dims:
        half = terms[0].shape[0] // 2
        send = functools.reduce(jnp.add, [t[half : 2 * half] for t in terms])
        terms = [t[:half] for t in terms] + [swap(send, "particle", dim)]
    return functools.reduce(jnp.add, [t[0] for t in terms])


def ring_sum(value, axis, first, second):
    a, b, c = (swap(value, axis, m) for m in (first, second, first ^ second))
    return (value + a) + (b + c)


def local(residuals, loadings):
    res, load = residuals[0], loadings[0]
    factor = (res.shape[0] * lax.axis_size("particle")) ** -0.5

    res, load = (pltpu.with_memory_space_constraint(v, pltpu.HBM) for v in (res, load))
    far, res, load, lh, ll = scores_far(res, load)
    got = swap(far, "coeffici", CORE)
    near = scores_near(res, lh, ll)

    p1 = swap(near[0, 2:] + got[0, 2:], "coeffici", X1)
    q1 = swap(near[1, 2:] + got[1, 2:], "coeffici", X2)
    p2 = swap(near[0, 1] + got[0, 1] + p1[1], "coeffici", X2)
    q2 = swap(near[1, 1] + got[1, 1] + q1[1], "coeffici", X1)
    own_p, own_q = own_block(near, got, p1, p2, q1, q2)

    a_p, a_q = swap(own_p, "coeffici", X2), swap(own_q, "coeffici", X1)
    b_p = swap(jnp.stack([own_p, a_p]), "coeffici", X1)
    b_q = swap(jnp.stack([own_q, a_q]), "coeffici", X2)
    far = swap(jnp.concatenate([jnp.stack([own_p, a_p, own_q, a_q]), b_p, b_q]), "coeffici", CORE)

    st, part_p = covariance_first(res, own_p, own_q, a_p, a_q, b_p, b_q, far)
    part_q = covariance_second(res, st)
    mine = jnp.stack([reduce_half(v, order) for v, order in zip((part_p, part_q), ORDERS)])
    other = swap(mine, "half", 1)
    w, corr = shrink(factor, load, mine, other)

    corr = corr[0] + swap(corr[1], "coeffici", CORE)
    corr = ring_sum(corr, "coeffici", X1, X2)
    groups = [[4 * y + z for z in range(4)] for y in range(4)]
    terms = lax.all_to_all(jnp.stack([corr] * 4), "particle", 0, 0, axis_index_groups=groups)
    corr = (terms[0] + terms[1]) + (terms[2] + terms[3])
    far0 = swap(corr, "coeffici", CORE)
    got = [swap(jnp.stack([corr, w[n]]), "particle", m) for n, m in ((1, Y1), (2, Y2), (3, Y1 ^ Y2))]
    far = swap(jnp.stack([g[0] for g in got]), "coeffici", CORE)
    weighted, rayleigh = assemble(w, corr, *got, far0, far)
    return weighted[None], rayleigh[None]


def solution(mesh):
    in_specs = (P("half", "particle", "coeffici"), P("half", "coeffici", None))
    out_specs = (P("half", ("coeffici", "particle"), None), P("half", None, None))
    return jax.shard_map(local, mesh=mesh, in_specs=in_specs, out_specs=out_specs, check_vma=False)
```

```python
import functools

import jax
import jax.numpy as jnp
from jax import lax
from jax.experimental import pallas as pl
from jax.experimental.pallas import tpu as pltpu
from jax.sharding import PartitionSpec as P


F32 = jnp.float32
BF16 = jnp.bfloat16
VMEM = pl.BlockSpec(memory_space=pltpu.VMEM)
HBM = pl.BlockSpec(memory_space=pltpu.HBM)
LANE = 128

RING = (0, 1, 3, 2)
CORE, X, Y, Z = 1, 2, 4, 1
PLACES = ((0, 3, 1, 2), (0, 1, 3, 2))


def swap(value, axis, mask):
    return lax.ppermute(value, axis, [(s, s ^ mask) for s in range(lax.axis_size(axis))])


def split(value):
    high = value.astype(BF16)
    return high, (value - high.astype(F32)).astype(BF16)


def dot(left, right):
    return lax.dot_general(left, right, (((1,), (0,)), ((), ())), preferred_element_type=F32)


def dot3(lh, ll, rh, rl):
    return dot(lh, rh) + dot(ll, rh) + dot(lh, rl)


def at(index, size):
    return pl.ds(pl.multiple_of(index * size, size), size)


def params(mib):
    return pltpu.CompilerParams(vmem_limit_bytes=mib << 20)


def shape(*dims, dtype=F32):
    return jax.ShapeDtypeStruct(dims, dtype)


def cost(flops, mib):
    return pl.CostEstimate(flops=flops, bytes_accessed=mib << 20, transcendentals=0)


def scores_kernel(side, *refs):
    if side:
        res, load, out, rh, rl, lh, ll, rbuf, lbuf, acc, rsems, lsems = refs
    else:
        res, lh, ll, out, rh, rl, rbuf, acc, rsems = refs
    me = lax.axis_index("coeffici")
    core = me & 1
    size = out.shape[1]
    depth = lh.shape[0] // 4
    copies = []
    for step in range(4):
        cols = slice(step * depth, (step + 1) * depth)
        some = []
        if side:
            some.append(pltpu.make_async_copy(load.at[cols], lbuf.at[cols], lsems.at[step]))
        for t in range(4):
            rows = at(2 * t + (core ^ side), size)
            some.append(pltpu.make_async_copy(res.at[rows, cols], rbuf.at[pl.ds(t * size, size), cols], rsems.at[step, t]))
        for copy in some:
            copy.start()
        copies.append(some)
    for step in range(4):
        for copy in copies[step]:
            copy.wait()
        cols = slice(step * depth, (step + 1) * depth)
        if side:
            lh[cols], ll[cols] = split(lbuf[cols])
        high, low = split(rbuf[:, cols])
        rh[:, cols], rl[:, cols] = high, low
        term = dot3(high, low, lh[cols], ll[cols])
        if step == 0:
            acc[...] = term
        else:
            acc[...] += term
    for t in range(4):
        mask = (me ^ (2 * t + (core ^ side))) >> 1
        out[mask ^ (mask >> 1)] = acc[t * size : (t + 1) * size]


def scores(side, res, *load):
    rows, coefs = res.shape
    k = load[0].shape[1]
    operand = shape(rows // 2, coefs, dtype=BF16)
    loads = (shape(coefs, k, dtype=BF16),) * 2
    lbuf = [pltpu.VMEM((coefs, k), F32)]
    return pl.pallas_call(
        functools.partial(scores_kernel, side),
        out_shape=(shape(4, rows // 8, k), operand, operand) + (loads if side else ()),
        in_specs=[HBM, HBM] if side else [HBM, VMEM, VMEM],
        out_specs=(VMEM,) * (5 if side else 3),
        scratch_shapes=[pltpu.VMEM((rows // 2, coefs), F32)]
        + (lbuf if side else [])
        + [pltpu.VMEM((rows // 2, k), F32), pltpu.SemaphoreType.DMA((4, 4))]
        + ([pltpu.SemaphoreType.DMA((4,))] if side else []),
        compiler_params=params(20),
        cost_estimate=cost(3 * rows * coefs * k, 6),
        name="scores_far" if side else "scores_near",
    )(res, *load)


def own_kernel(near, got, r1, r2, r3, out):
    out[...] = ((near[0] + got[0]) + (r1[...] + r2[...]) + r3[...]).T


def own_block(*terms):
    _, rows, k = terms[0].shape
    return pl.pallas_call(
        own_kernel,
        out_shape=shape(k, rows),
        in_specs=[VMEM] * 5,
        out_specs=VMEM,
        compiler_params=params(4),
        cost_estimate=cost(1 << 18, 1),
        name="own_block",
    )(*terms)


def stage_kernel(*refs):
    pieces, out = refs[:-1], refs[-1]
    me = lax.axis_index("coeffici")
    for n in range(4):
        piece = pieces[n][...] if len(pieces) == 4 else pieces[0][n]
        high, low = split(piece)
        where = at((me ^ (X * RING[n])) >> 1, LANE)
        for block in range(4):
            rows = slice(64 * block, 64 * block + 64)
            out[128 * block : 128 * block + 64, where] = high[rows]
            out[128 * block + 64 : 128 * block + 128, where] = low[rows]


def stage(*pieces):
    return pl.pallas_call(
        stage_kernel,
        out_shape=shape(4 * LANE, 4 * LANE, dtype=BF16),
        in_specs=[VMEM] * len(pieces),
        out_specs=VMEM,
        compiler_params=params(4),
        cost_estimate=cost(1 << 18, 1),
        name="stage",
    )(*pieces)


def covariance_kernel(jobs, *refs):
    ops, outs = refs[:6], refs[6:]
    particle = lax.axis_index("particle")
    y, z = particle >> 2, particle & 3
    for (part, places), out in zip(jobs, outs):
        blocks = [y ^ PLACES[part][place] for place in places]

        @pl.loop(0, 4)
        def _(zp):
            column = z ^ zp ^ (zp >> 1)
            both = low = None
            for st, rh, rl in (ops[:3], ops[3:]):
                pick = [at(4 * (2 * part + n) + column, LANE) for n in range(2)]
                high = jnp.concatenate([rh[:, p] for p in pick], axis=1)
                rest = jnp.concatenate([rl[:, p] for p in pick], axis=1)
                left = jnp.concatenate([st[at(b, LANE)] for b in blocks])
                left_high = jnp.concatenate([st[pl.ds(pl.multiple_of(b * LANE, LANE), 64)] for b in blocks])
                first, second = dot(left, high), dot(left_high, rest)
                both = first if both is None else both + first
                low = second if low is None else low + second
            for n in range(2):
                top = LANE * n
                out[4 * n + zp] = both[top : top + 64] + both[top + 64 : top + LANE] + low[64 * n : 64 * n + 64]


def covariance(jobs, operands, name):
    rows, coefs = operands[1].shape
    return pl.pallas_call(
        functools.partial(covariance_kernel, jobs),
        out_shape=tuple(shape(8, 64, 2 * LANE) for _ in jobs),
        in_specs=[VMEM] * 6,
        out_specs=(VMEM,) * len(jobs),
        compiler_params=params(16),
        cost_estimate=cost(3 * rows * coefs * LANE * len(jobs), 4),
        name=name,
    )(*operands)


def shrink_kernel(factor, load_h, load_l, mine, other, w_out, corr_out, cbuf):
    particle = lax.axis_index("particle")
    y, z = particle >> 2, particle & 3
    core = lax.axis_index("coeffici") & 1
    corr = None
    for n in range(4):
        cols = slice((n & 1) * LANE, (n & 1) * LANE + LANE)
        cov = mine[n >> 1, :, cols] * factor
        far = other[n >> 1, :, cols] * factor
        weighted = cov * jax.nn.sigmoid(cov * far)
        mask = y ^ n
        w_out[mask ^ (mask >> 1)] = weighted
        wh, wl = split(weighted)
        where = at(4 * n + z, LANE)
        term = dot3(wh, wl, load_h[where], load_l[where])
        corr = term if corr is None else corr + term
    cbuf[...] = corr * factor
    for n in range(2):
        rows = cbuf[at(core ^ n, 32)]
        corr_out[n, :32] = rows[:, :LANE]
        corr_out[n, 32:] = rows[:, LANE:]


def shrink(factor, *args):
    return pl.pallas_call(
        functools.partial(shrink_kernel, factor),
        out_shape=(shape(4, 64, LANE), shape(2, 64, LANE)),
        in_specs=[VMEM] * 4,
        out_specs=(VMEM, VMEM),
        scratch_shapes=[pltpu.VMEM((64, 2 * LANE), F32)],
        compiler_params=params(8),
        cost_estimate=cost(6 * 64 * 512 * 256, 1),
        name="shrink",
    )(*args)


def assemble_kernel(w, corr, r1, r2, r3, far0, far, w_out, corr_out, wbuf, cbuf):
    y = lax.axis_index("particle") >> 2
    core = lax.axis_index("coeffici") & 1
    got = (None, r1, r2, r3)
    for n in range(4):
        block = y ^ RING[n]
        wbuf[at(block, 64)] = w[0] if n == 0 else got[n][1]
        for c in range(2):
            if n == 0:
                piece = (corr if c == 0 else far0)[...]
            else:
                piece = got[n][0] if c == 0 else far[n - 1]
            where = at(2 * block + (core ^ c), 32)
            cbuf[where, :LANE] = piece[:32]
            cbuf[where, LANE:] = piece[32:]
    w_out[...] = wbuf[...].T
    corr_out[...] = cbuf[...].T


def assemble(*args):
    k = 2 * LANE
    return pl.pallas_call(
        assemble_kernel,
        out_shape=(shape(LANE, k), shape(k, k)),
        in_specs=[VMEM] * len(args),
        out_specs=(VMEM, VMEM),
        scratch_shapes=[pltpu.VMEM((k, LANE), F32), pltpu.VMEM((k, k), F32)],
        compiler_params=params(4),
        name="assemble",
    )(*args)


def ring_swap(values, axis, unit):
    return [swap(v, axis, unit * m) for v, m in zip(values, RING[1:])]


def ring_sum(value, axis, unit):
    a, b, c = ring_swap([value] * 3, axis, unit)
    return (value + a) + (b + c)


def local(residuals, loadings):
    res, load = (pltpu.with_memory_space_constraint(v[0], pltpu.HBM) for v in (residuals, loadings))
    factor = (res.shape[0] * lax.axis_size("particle")) ** -0.5

    far, fh, fl, lh, ll = scores(1, res, load)
    got = swap(far, "coeffici", CORE)
    near, nh, nl = scores(0, res, lh, ll)
    own = own_block(near, got, *ring_swap([near[n] + got[n] for n in (1, 2, 3)], "coeffici", X))
    pieces = [own] + ring_swap([own] * 3, "coeffici", X)
    others = swap(jnp.stack(pieces), "coeffici", CORE)
    operands = (stage(*pieces), nh, nl, stage(others), fh, fl)

    (leave_p,) = covariance(((0, (2, 3)),), operands, "covariance_p")
    one_p = swap(leave_p, "particle", Y)
    (leave_q,) = covariance(((1, (2, 3)),), operands, "covariance_q")
    one_q = swap(leave_q, "particle", 3 * Y)
    keep_p, keep_q = covariance(((0, (0, 1)), (1, (0, 1))), operands, "covariance_keep")
    two_p = swap(keep_p[4:] + one_p[4:], "particle", 3 * Y)
    two_q = swap(keep_q[4:] + one_q[4:], "particle", Y)

    def at_z(n):
        return jnp.stack([keep_p[n] + one_p[n] + two_p[n], keep_q[n] + one_q[n] + two_q[n]])

    r1, r2, r3 = ring_swap([at_z(n) for n in (1, 2, 3)], "particle", Z)
    mine = at_z(0) + (r1 + r2) + r3
    other = swap(mine, "half", 1)
    w, corr = shrink(factor, lh, ll, mine, other)

    corr = corr[0] + swap(corr[1], "coeffici", CORE)
    corr = ring_sum(corr, "coeffici", X)
    corr = ring_sum(corr, "particle", Z)
    far0 = swap(corr, "coeffici", CORE)
    got = ring_swap([jnp.stack([corr, w[n]]) for n in (1, 2, 3)], "particle", Y)
    far = swap(jnp.stack([g[0] for g in got]), "coeffici", CORE)
    weighted, rayleigh = assemble(w, corr, *got, far0, far)
    return weighted[None], rayleigh[None]


def solution(mesh):
    in_specs = (P("half", "particle", "coeffici"), P("half", "coeffici", None))
    out_specs = (P("half", ("coeffici", "particle"), None), P("half", None, None))
    return jax.shard_map(local, mesh=mesh, in_specs=in_specs, out_specs=out_specs, check_vma=False)
```

```python
import functools

import jax
import jax.numpy as jnp
from jax import lax
from jax.experimental import pallas as pl
from jax.experimental.pallas import tpu as pltpu
from jax.sharding import PartitionSpec as P


F32 = jnp.float32
BF16 = jnp.bfloat16
VMEM = pl.BlockSpec(memory_space=pltpu.VMEM)
HBM = pl.BlockSpec(memory_space=pltpu.HBM)
LANE = 128

RING = (0, 1, 3, 2)
CORE, X, Y, Z = 1, 2, 4, 1
PLACES = ((0, 3, 1, 2), (0, 1, 3, 2))


def swap(value, axis, mask):
    return lax.ppermute(value, axis, [(s, s ^ mask) for s in range(lax.axis_size(axis))])


def split(value):
    high = value.astype(BF16)
    return high, (value - high.astype(F32)).astype(BF16)


def dot(left, right):
    return lax.dot_general(left, right, (((1,), (0,)), ((), ())), preferred_element_type=F32)


def dot3(lh, ll, rh, rl):
    return dot(lh, rh) + dot(ll, rh) + dot(lh, rl)


def at(index, size):
    return pl.ds(pl.multiple_of(index * size, size), size)


def params(mib):
    return pltpu.CompilerParams(vmem_limit_bytes=mib << 20)


def shape(*dims, dtype=F32):
    return jax.ShapeDtypeStruct(dims, dtype)


def cost(flops, mib):
    return pl.CostEstimate(flops=flops, bytes_accessed=mib << 20, transcendentals=0)


def scores_kernel(side, *refs):
    if side:
        res, load, out, rh, rl, lh, ll, later, rbuf, lbuf, acc, rsems, lsems, nsems = refs
    else:
        rbuf, lh, ll, out, rh, rl, acc = refs
    me = lax.axis_index("coeffici")
    core = me & 1
    size = out.shape[1]
    depth = lh.shape[0] // 4
    copies, others = [[] for _ in range(4)], []
    if side:
        for step in range(4):
            cols = slice(step * depth, (step + 1) * depth)
            copies[step].append(pltpu.make_async_copy(load.at[cols], lbuf.at[cols], lsems.at[step]))
            for t in range(4):
                copies[step].append(
                    pltpu.make_async_copy(
                        res.at[at(2 * t + (core ^ 1), size), cols], rbuf.at[pl.ds(t * size, size), cols], rsems.at[step, t]
                    )
                )
        for t in range(4):
            others.append(
                pltpu.make_async_copy(res.at[at(2 * t + core, size)], later.at[pl.ds(t * size, size)], nsems.at[t])
            )
        for copy in sum(copies, []) + others:
            copy.start()
    for step in range(4):
        for copy in copies[step]:
            copy.wait()
        cols = slice(step * depth, (step + 1) * depth)
        if side:
            lh[cols], ll[cols] = split(lbuf[cols])
        high, low = split(rbuf[:, cols])
        rh[:, cols], rl[:, cols] = high, low
        term = dot3(high, low, lh[cols], ll[cols])
        if step == 0:
            acc[...] = term
        else:
            acc[...] += term
    for t in range(4):
        mask = (me ^ (2 * t + (core ^ side))) >> 1
        out[mask ^ (mask >> 1)] = acc[t * size : (t + 1) * size]
    for copy in others:
        copy.wait()


def scores(side, res, *load):
    rows, coefs = res.shape
    rows = rows if side else 2 * rows
    k = load[0].shape[1]
    operand = shape(rows // 2, coefs, dtype=BF16)
    extra = (shape(coefs, k, dtype=BF16),) * 2 + (shape(rows // 2, coefs),)
    acc = pltpu.VMEM((rows // 2, k), F32)
    dma = pltpu.SemaphoreType.DMA
    return pl.pallas_call(
        functools.partial(scores_kernel, side),
        out_shape=(shape(4, rows // 8, k), operand, operand) + (extra if side else ()),
        in_specs=[HBM, HBM] if side else [VMEM] * 3,
        out_specs=(VMEM,) * (6 if side else 3),
        scratch_shapes=[pltpu.VMEM((rows // 2, coefs), F32), pltpu.VMEM((coefs, k), F32), acc, dma((4, 4)), dma((4,)), dma((4,))]
        if side
        else [acc],
        compiler_params=params(20),
        cost_estimate=cost(3 * rows * coefs * k, 6),
        name="scores_far" if side else "scores_near",
    )(res, *load)


def own_kernel(near, got, r1, r2, r3, out):
    out[...] = ((near[0] + got[0]) + (r1[...] + r2[...]) + r3[...]).T


def own_block(*terms):
    _, rows, k = terms[0].shape
    return pl.pallas_call(
        own_kernel,
        out_shape=shape(k, rows),
        in_specs=[VMEM] * 5,
        out_specs=VMEM,
        compiler_params=params(4),
        cost_estimate=cost(1 << 18, 1),
        name="own_block",
    )(*terms)


def stage_kernel(*refs):
    pieces, out = refs[:-1], refs[-1]
    me = lax.axis_index("coeffici")
    for n in range(4):
        piece = pieces[n][...] if len(pieces) == 4 else pieces[0][n]
        high, low = split(piece)
        where = at((me ^ (X * RING[n])) >> 1, LANE)
        for block in range(4):
            rows = slice(64 * block, 64 * block + 64)
            out[128 * block : 128 * block + 64, where] = high[rows]
            out[128 * block + 64 : 128 * block + 128, where] = low[rows]


def stage(*pieces):
    return pl.pallas_call(
        stage_kernel,
        out_shape=shape(4 * LANE, 4 * LANE, dtype=BF16),
        in_specs=[VMEM] * len(pieces),
        out_specs=VMEM,
        compiler_params=params(4),
        cost_estimate=cost(1 << 18, 1),
        name="stage",
    )(*pieces)


def columns(refs, ys, zs):
    return [jnp.concatenate([r[:, at(4 * y + z, LANE)] for z in zs for y in ys], axis=1) for r in refs]


def pair_kernel(places, sides, add, *refs):
    ops, before, (out_p, out_q) = refs[: 3 * sides], refs[3 * sides : 3 * sides + 2 * add], refs[-2:]
    particle = lax.axis_index("particle")
    y, z = particle >> 2, particle & 3
    starts = [(y ^ PLACES[part][place]) * LANE + 32 * part for part in range(2) for place in places]
    starts += [s + 64 for s in starts]
    wide = out_p.shape[2]

    @pl.loop(0, 2)
    def _(step):
        spots = [2 * step, 2 * step + 1]
        total = None
        for side in range(sides):
            st, rh, rl = ops[3 * side : 3 * side + 3]
            high, rest = columns((rh, rl), range(3), [z ^ s ^ (s >> 1) for s in spots])
            left = jnp.concatenate([st[pl.ds(pl.multiple_of(s, 32), 32)] for s in starts])
            both, low = dot(left, high), dot(left[:LANE], rest)
            term = both[:LANE] + both[LANE:] + low
            total = term if total is None else total + term
        for part, out in enumerate((out_p, out_q)):
            for n in range(2):
                for i, spot in enumerate(spots):
                    top = 64 * part + 32 * n
                    value = total[top : top + 32, wide * i : wide * (i + 1)]
                    if add:
                        value = value + before[part][4 * n + spot]
                    out[4 * n + spot] = value


def covariance_pair(places, operands, before):
    rows, coefs = operands[1].shape
    sides = len(operands) // 3
    out = shape(8, 32, 3 * LANE)
    return pl.pallas_call(
        functools.partial(pair_kernel, places, sides, len(before) // 2),
        out_shape=(out, out),
        in_specs=[VMEM] * (len(operands) + len(before)),
        out_specs=(VMEM, VMEM),
        compiler_params=params(16),
        cost_estimate=cost(3 * rows * coefs * LANE * sides, 4),
    )(*operands, *before)


def third_kernel(*refs):
    ops, out = refs[:6], refs[6]
    particle = lax.axis_index("particle")
    y, z = particle >> 2, particle & 3

    @pl.loop(0, 2)
    def _(step):
        spots = [2 * step, 2 * step + 1]
        both = low = None
        for st, rh, rl in (ops[:3], ops[3:]):
            high, rest = columns((rh, rl), [3], [z ^ s ^ (s >> 1) for s in spots])
            left_high = jnp.concatenate([st[LANE * b : LANE * b + 64] for b in range(4)])
            first, second = dot(st[...], high), dot(left_high, rest)
            both = first if both is None else both + first
            low = second if low is None else low + second
        for b in range(4):
            mask = y ^ b
            place = mask ^ (mask >> 1)
            top = LANE * b
            value = both[top : top + 64] + both[top + 64 : top + LANE] + low[64 * b : 64 * b + 64]
            for i, spot in enumerate(spots):
                out[4 * spot + place] = value[:, LANE * i : LANE * (i + 1)]


def covariance_third(operands):
    rows, coefs = operands[1].shape
    return pl.pallas_call(
        third_kernel,
        out_shape=shape(16, 64, LANE),
        in_specs=[VMEM] * 6,
        out_specs=VMEM,
        compiler_params=params(16),
        cost_estimate=cost(3 * rows * coefs * LANE, 4),
        name="covariance_third",
    )(*operands)


def shrink_kernel(factor, load_h, load_l, mine, other, w_out, corr_out, cbuf):
    particle = lax.axis_index("particle")
    y, z = particle >> 2, particle & 3
    core = lax.axis_index("coeffici") & 1
    corr = None
    for n in range(4):
        cols = slice(n * LANE, n * LANE + LANE)
        cov = mine[:, cols] * factor
        far = other[:, cols] * factor
        weighted = cov * jax.nn.sigmoid(cov * far)
        mask = y ^ n
        w_out[mask ^ (mask >> 1)] = weighted
        wh, wl = split(weighted)
        where = at(4 * n + z, LANE)
        term = dot3(wh, wl, load_h[where], load_l[where])
        corr = term if corr is None else corr + term
    cbuf[...] = corr * factor
    for n in range(2):
        rows = cbuf[at(core ^ n, 32)]
        corr_out[n, :32] = rows[:, :LANE]
        corr_out[n, 32:] = rows[:, LANE:]


def shrink(factor, *args):
    return pl.pallas_call(
        functools.partial(shrink_kernel, factor),
        out_shape=(shape(4, 64, LANE), shape(2, 64, LANE)),
        in_specs=[VMEM] * 4,
        out_specs=(VMEM, VMEM),
        scratch_shapes=[pltpu.VMEM((64, 2 * LANE), F32)],
        compiler_params=params(8),
        cost_estimate=cost(6 * 64 * 512 * 256, 1),
        name="shrink",
    )(*args)


def assemble_kernel(w, corr, r1, r2, r3, far0, far, w_out, corr_out, wbuf, cbuf):
    y = lax.axis_index("particle") >> 2
    core = lax.axis_index("coeffici") & 1
    got = (None, r1, r2, r3)
    for n in range(4):
        block = y ^ RING[n]
        wbuf[at(block, 64)] = w[0] if n == 0 else got[n][1]
        for c in range(2):
            if n == 0:
                piece = (corr if c == 0 else far0)[...]
            else:
                piece = got[n][0] if c == 0 else far[n - 1]
            where = at(2 * block + (core ^ c), 32)
            cbuf[where, :LANE] = piece[:32]
            cbuf[where, LANE:] = piece[32:]
    w_out[...] = wbuf[...].T
    corr_out[...] = cbuf[...].T


def assemble(*args):
    k = 2 * LANE
    return pl.pallas_call(
        assemble_kernel,
        out_shape=(shape(LANE, k), shape(k, k)),
        in_specs=[VMEM] * len(args),
        out_specs=(VMEM, VMEM),
        scratch_shapes=[pltpu.VMEM((k, LANE), F32), pltpu.VMEM((k, k), F32)],
        compiler_params=params(4),
        name="assemble",
    )(*args)


def ring_swap(values, axis, unit):
    return [swap(v, axis, unit * m) for v, m in zip(values, RING[1:])]


def ring_sum(value, axis, unit):
    a, b, c = ring_swap([value] * 3, axis, unit)
    return (value + a) + (b + c)


def step(residuals, loadings):
    res, load = (pltpu.with_memory_space_constraint(v[0], pltpu.HBM) for v in (residuals, loadings))
    factor = (res.shape[0] * lax.axis_size("particle")) ** -0.5

    far, fh, fl, lh, ll, rest = scores(1, res, load)
    got = swap(far, "coeffici", CORE)
    near, nh, nl = scores(0, rest, lh, ll)
    own = own_block(near, got, *ring_swap([near[n] + got[n] for n in (1, 2, 3)], "coeffici", X))
    pieces = [own] + ring_swap([own] * 3, "coeffici", X)
    others = swap(jnp.stack(pieces), "coeffici", CORE)
    near_ops = (stage(*pieces), nh, nl)
    far_ops = (stage(others), fh, fl)

    leave = covariance_pair((2, 3), near_ops, ())
    leave_p, leave_q = covariance_pair((2, 3), far_ops, leave)
    one_p = swap(leave_p, "particle", Y)
    one_q = swap(leave_q, "particle", 3 * Y)
    third = covariance_third(near_ops + far_ops)
    sums = ring_swap([third[4 * n : 4 * n + 4] for n in (1, 2, 3)], "particle", Z)
    keep_p, keep_q = covariance_pair((0, 1), near_ops + far_ops, ())
    two_p = swap(keep_p[4:] + one_p[4:], "particle", 3 * Y)
    two_q = swap(keep_q[4:] + one_q[4:], "particle", Y)

    def at_z(n):
        return jnp.concatenate([keep_p[n] + one_p[n] + two_p[n], keep_q[n] + one_q[n] + two_q[n]])

    def at_y(n):
        return third[n] + (sums[0][n] + sums[1][n]) + sums[2][n]

    r1, r2, r3 = ring_swap([at_z(n) for n in (1, 2, 3)], "particle", Z)
    t1, t2, t3 = ring_swap([at_y(n) for n in (1, 2, 3)], "particle", Y)
    mine = jnp.concatenate([at_z(0) + (r1 + r2) + r3, at_y(0) + (t1 + t2) + t3], axis=1)
    other = swap(mine, "half", 1)
    w, corr = shrink(factor, lh, ll, mine, other)

    corr = corr[0] + swap(corr[1], "coeffici", CORE)
    corr = ring_sum(corr, "coeffici", X)
    corr = ring_sum(corr, "particle", Z)
    far0 = swap(corr, "coeffici", CORE)
    got = ring_swap([jnp.stack([corr, w[n]]) for n in (1, 2, 3)], "particle", Y)
    far = swap(jnp.stack([g[0] for g in got]), "coeffici", CORE)
    weighted, rayleigh = assemble(w, corr, *got, far0, far)
    return weighted[None], rayleigh[None]


def solution(mesh):
    in_specs = (P("half", "particle", "coeffici"), P("half", "coeffici", None))
    out_specs = (P("half", ("coeffici", "particle"), None), P("half", None, None))
    return jax.shard_map(step, mesh=mesh, in_specs=in_specs, out_specs=out_specs, check_vma=False)
```

```python
import functools

import jax
import jax.numpy as jnp
from jax import lax
from jax.experimental import pallas as pl
from jax.experimental.pallas import tpu as pltpu
from jax.sharding import PartitionSpec as P


F32 = jnp.float32
BF16 = jnp.bfloat16
VMEM = pl.BlockSpec(memory_space=pltpu.VMEM)
HBM = pl.BlockSpec(memory_space=pltpu.HBM)
LANE = 128

RING = (0, 1, 3, 2)
CORE, X, Y, Z = 1, 2, 4, 1
PLACES = ((0, 3, 1, 2), (0, 1, 3, 2))


def swap(value, axis, mask):
    return lax.ppermute(value, axis, [(s, s ^ mask) for s in range(lax.axis_size(axis))])


def split(value):
    high = value.astype(BF16)
    return high, (value - high.astype(F32)).astype(BF16)


def dot(left, right):
    return lax.dot_general(left, right, (((1,), (0,)), ((), ())), preferred_element_type=F32)


def dot3(lh, ll, rh, rl):
    return dot(lh, rh) + dot(ll, rh) + dot(lh, rl)


def at(index, size):
    return pl.ds(pl.multiple_of(index * size, size), size)


def params(mib):
    return pltpu.CompilerParams(vmem_limit_bytes=mib << 20)


def shape(*dims, dtype=F32):
    return jax.ShapeDtypeStruct(dims, dtype)


def cost(flops, mib):
    return pl.CostEstimate(flops=flops, bytes_accessed=mib << 20, transcendentals=0)


def scores_kernel(side, *refs):
    if side:
        res, load, out, rh, rl, lh, ll, later, rbuf, lbuf, acc, rsems, lsems, nsems = refs
    else:
        rbuf, lh, ll, out, rh, rl, acc = refs
    me = lax.axis_index("coeffici")
    core = me & 1
    size = out.shape[1]
    depth = lh.shape[0] // 4
    copies, others = [[] for _ in range(4)], []
    if side:
        for step in range(4):
            cols = slice(step * depth, (step + 1) * depth)
            copies[step].append(pltpu.make_async_copy(load.at[cols], lbuf.at[cols], lsems.at[step]))
            for t in range(4):
                copies[step].append(
                    pltpu.make_async_copy(
                        res.at[at(2 * t + (core ^ 1), size), cols], rbuf.at[pl.ds(t * size, size), cols], rsems.at[step, t]
                    )
                )
        for t in range(4):
            others.append(
                pltpu.make_async_copy(res.at[at(2 * t + core, size)], later.at[pl.ds(t * size, size)], nsems.at[t])
            )
        for copy in copies[0] + copies[1]:
            copy.start()
    for step in range(4):
        for copy in copies[step]:
            copy.wait()
        for copy in (copies[2], copies[3] + others[:1], others[1:], ())[step] if side else ():
            copy.start()
        cols = slice(step * depth, (step + 1) * depth)
        if side:
            lh[cols], ll[cols] = split(lbuf[cols])
        high, low = split(rbuf[:, cols])
        rh[:, cols], rl[:, cols] = high, low
        term = dot3(high, low, lh[cols], ll[cols])
        if step == 0:
            acc[...] = term
        else:
            acc[...] += term
    for t in range(4):
        mask = (me ^ (2 * t + (core ^ side))) >> 1
        out[mask ^ (mask >> 1)] = acc[t * size : (t + 1) * size]
    for copy in others:
        copy.wait()


def scores(side, res, *load):
    rows, coefs = res.shape
    rows = rows if side else 2 * rows
    k = load[0].shape[1]
    operand = shape(rows // 2, coefs, dtype=BF16)
    extra = (shape(coefs, k, dtype=BF16),) * 2 + (shape(rows // 2, coefs),)
    acc = pltpu.VMEM((rows // 2, k), F32)
    dma = pltpu.SemaphoreType.DMA
    return pl.pallas_call(
        functools.partial(scores_kernel, side),
        out_shape=(shape(4, rows // 8, k), operand, operand) + (extra if side else ()),
        in_specs=[HBM, HBM] if side else [VMEM] * 3,
        out_specs=(VMEM,) * (6 if side else 3),
        scratch_shapes=[pltpu.VMEM((rows // 2, coefs), F32), pltpu.VMEM((coefs, k), F32), acc, dma((4, 4)), dma((4,)), dma((4,))]
        if side
        else [acc],
        compiler_params=params(20),
        cost_estimate=cost(3 * rows * coefs * k, 6),
        name="scores_far" if side else "scores_near",
    )(res, *load)


def own_kernel(near, got, r1, r2, r3, out):
    out[...] = ((near[0] + got[0]) + (r1[...] + r2[...]) + r3[...]).T


def own_block(*terms):
    _, rows, k = terms[0].shape
    return pl.pallas_call(
        own_kernel,
        out_shape=shape(k, rows),
        in_specs=[VMEM] * 5,
        out_specs=VMEM,
        compiler_params=params(4),
        cost_estimate=cost(1 << 18, 1),
        name="own_block",
    )(*terms)


def stage_kernel(*refs):
    pieces, out = refs[:-1], refs[-1]
    me = lax.axis_index("coeffici")
    for n in range(4):
        piece = pieces[n][...] if len(pieces) == 4 else pieces[0][n]
        high, low = split(piece)
        where = at((me ^ (X * RING[n])) >> 1, LANE)
        for block in range(4):
            rows = slice(64 * block, 64 * block + 64)
            out[128 * block : 128 * block + 64, where] = high[rows]
            out[128 * block + 64 : 128 * block + 128, where] = low[rows]


def stage(*pieces):
    return pl.pallas_call(
        stage_kernel,
        out_shape=shape(4 * LANE, 4 * LANE, dtype=BF16),
        in_specs=[VMEM] * len(pieces),
        out_specs=VMEM,
        compiler_params=params(4),
        cost_estimate=cost(1 << 18, 1),
        name="stage",
    )(*pieces)


def columns(refs, ys, zs):
    return [jnp.concatenate([r[:, at(4 * y + z, LANE)] for z in zs for y in ys], axis=1) for r in refs]


def pair_kernel(places, sides, add, *refs):
    ops, before, (out_p, out_q) = refs[: 3 * sides], refs[3 * sides : 3 * sides + 2 * add], refs[-2:]
    particle = lax.axis_index("particle")
    y, z = particle >> 2, particle & 3
    starts = [(y ^ PLACES[part][place]) * LANE + 32 * part for part in range(2) for place in places]
    starts += [s + 64 for s in starts]
    wide = out_p.shape[2]

    @pl.loop(0, 2)
    def _(step):
        spots = [2 * step, 2 * step + 1]
        total = None
        for side in range(sides):
            st, rh, rl = ops[3 * side : 3 * side + 3]
            high, rest = columns((rh, rl), range(3), [z ^ s ^ (s >> 1) for s in spots])
            left = jnp.concatenate([st[pl.ds(pl.multiple_of(s, 32), 32)] for s in starts])
            both, low = dot(left, high), dot(left[:LANE], rest)
            term = both[:LANE] + both[LANE:] + low
            total = term if total is None else total + term
        for part, out in enumerate((out_p, out_q)):
            for n in range(2):
                for i, spot in enumerate(spots):
                    top = 64 * part + 32 * n
                    value = total[top : top + 32, wide * i : wide * (i + 1)]
                    if add:
                        value = value + before[part][4 * n + spot]
                    out[4 * n + spot] = value


def covariance_pair(places, operands, before):
    rows, coefs = operands[1].shape
    sides = len(operands) // 3
    out = shape(8, 32, 3 * LANE)
    return pl.pallas_call(
        functools.partial(pair_kernel, places, sides, len(before) // 2),
        out_shape=(out, out),
        in_specs=[VMEM] * (len(operands) + len(before)),
        out_specs=(VMEM, VMEM),
        compiler_params=params(16),
        cost_estimate=cost(3 * rows * coefs * LANE * sides, 4),
    )(*operands, *before)


def third_kernel(*refs):
    ops, out = refs[:6], refs[6]
    particle = lax.axis_index("particle")
    y, z = particle >> 2, particle & 3

    @pl.loop(0, 2)
    def _(step):
        spots = [2 * step, 2 * step + 1]
        both = low = None
        for st, rh, rl in (ops[:3], ops[3:]):
            high, rest = columns((rh, rl), [3], [z ^ s ^ (s >> 1) for s in spots])
            left_high = jnp.concatenate([st[LANE * b : LANE * b + 64] for b in range(4)])
            first, second = dot(st[...], high), dot(left_high, rest)
            both = first if both is None else both + first
            low = second if low is None else low + second
        for b in range(4):
            mask = y ^ b
            place = mask ^ (mask >> 1)
            top = LANE * b
            value = both[top : top + 64] + both[top + 64 : top + LANE] + low[64 * b : 64 * b + 64]
            for i, spot in enumerate(spots):
                out[4 * spot + place] = value[:, LANE * i : LANE * (i + 1)]


def covariance_third(operands):
    rows, coefs = operands[1].shape
    return pl.pallas_call(
        third_kernel,
        out_shape=shape(16, 64, LANE),
        in_specs=[VMEM] * 6,
        out_specs=VMEM,
        compiler_params=params(16),
        cost_estimate=cost(3 * rows * coefs * LANE, 4),
        name="covariance_third",
    )(*operands)


def shrink_kernel(factor, load_h, load_l, mine, other, w_out, corr_out, cbuf):
    particle = lax.axis_index("particle")
    y, z = particle >> 2, particle & 3
    core = lax.axis_index("coeffici") & 1
    corr = None
    for n in range(4):
        cols = slice(n * LANE, n * LANE + LANE)
        cov = mine[:, cols] * factor
        far = other[:, cols] * factor
        weighted = cov * jax.nn.sigmoid(cov * far)
        mask = y ^ n
        w_out[mask ^ (mask >> 1)] = weighted
        wh, wl = split(weighted)
        where = at(4 * n + z, LANE)
        term = dot3(wh, wl, load_h[where], load_l[where])
        corr = term if corr is None else corr + term
    cbuf[...] = corr * factor
    for n in range(2):
        rows = cbuf[at(core ^ n, 32)]
        corr_out[n, :32] = rows[:, :LANE]
        corr_out[n, 32:] = rows[:, LANE:]


def shrink(factor, *args):
    return pl.pallas_call(
        functools.partial(shrink_kernel, factor),
        out_shape=(shape(4, 64, LANE), shape(2, 64, LANE)),
        in_specs=[VMEM] * 4,
        out_specs=(VMEM, VMEM),
        scratch_shapes=[pltpu.VMEM((64, 2 * LANE), F32)],
        compiler_params=params(8),
        cost_estimate=cost(6 * 64 * 512 * 256, 1),
        name="shrink",
    )(*args)


def place_kernel(w, r1, r2, r3, out, buf):
    y = lax.axis_index("particle") >> 2
    for mask, piece in zip(RING, (w[0], r1[1], r2[1], r3[1])):
        buf[at(y ^ mask, 64)] = piece
    out[...] = buf[...].T


def assemble_kernel(near0, r1, r2, r3, far0, far, out, buf):
    y = lax.axis_index("particle") >> 2
    core = lax.axis_index("coeffici") & 1
    near = (near0[...], r1[0], r2[0], r3[0])
    for n in range(4):
        for c, piece in enumerate((near[n], far0[...] if n == 0 else far[n - 1])):
            where = at(2 * (y ^ RING[n]) + (core ^ c), 32)
            buf[where, :LANE] = piece[:32]
            buf[where, LANE:] = piece[32:]
    out[...] = buf[...].T


def place(*args):
    return pl.pallas_call(
        place_kernel,
        out_shape=shape(LANE, 2 * LANE),
        in_specs=[VMEM] * len(args),
        out_specs=VMEM,
        scratch_shapes=[pltpu.VMEM((2 * LANE, LANE), F32)],
        compiler_params=params(4),
        cost_estimate=cost(1 << 18, 1),
        name="place",
    )(*args)


def assemble(*args):
    k = 2 * LANE
    return pl.pallas_call(
        assemble_kernel,
        out_shape=shape(k, k),
        in_specs=[VMEM] * len(args),
        out_specs=VMEM,
        scratch_shapes=[pltpu.VMEM((k, k), F32)],
        compiler_params=params(4),
        name="assemble",
    )(*args)


def ring_swap(values, axis, unit):
    return [swap(v, axis, unit * m) for v, m in zip(values, RING[1:])]


def ring_sum(value, axis, unit):
    a, b, c = ring_swap([value] * 3, axis, unit)
    return (value + a) + (b + c)


def step(residuals, loadings):
    res, load = (pltpu.with_memory_space_constraint(v[0], pltpu.HBM) for v in (residuals, loadings))
    factor = (res.shape[0] * lax.axis_size("particle")) ** -0.5

    far, fh, fl, lh, ll, rest = scores(1, res, load)
    got = swap(far, "coeffici", CORE)
    near, nh, nl = scores(0, rest, lh, ll)
    own = own_block(near, got, *ring_swap([near[n] + got[n] for n in (1, 2, 3)], "coeffici", X))
    pieces = [own] + ring_swap([own] * 3, "coeffici", X)
    others = swap(jnp.stack(pieces), "coeffici", CORE)
    near_ops = (stage(*pieces), nh, nl)
    far_ops = (stage(others), fh, fl)

    leave = covariance_pair((2, 3), near_ops, ())
    leave_p, leave_q = covariance_pair((2, 3), far_ops, leave)
    one_p = swap(leave_p, "particle", Y)
    one_q = swap(leave_q, "particle", 3 * Y)
    third = covariance_third(near_ops + far_ops)
    sums = ring_swap([third[4 * n : 4 * n + 4] for n in (1, 2, 3)], "particle", Z)
    keep_p, keep_q = covariance_pair((0, 1), near_ops + far_ops, ())
    two_p = swap(keep_p[4:] + one_p[4:], "particle", 3 * Y)
    two_q = swap(keep_q[4:] + one_q[4:], "particle", Y)

    def at_z(n):
        return jnp.concatenate([keep_p[n] + one_p[n] + two_p[n], keep_q[n] + one_q[n] + two_q[n]])

    def at_y(n):
        return third[n] + (sums[0][n] + sums[1][n]) + sums[2][n]

    r1, r2, r3 = ring_swap([at_z(n) for n in (1, 2, 3)], "particle", Z)
    t1, t2, t3 = ring_swap([at_y(n) for n in (1, 2, 3)], "particle", Y)
    mine = jnp.concatenate([at_z(0) + (r1 + r2) + r3, at_y(0) + (t1 + t2) + t3], axis=1)
    other = swap(mine, "half", 1)
    w, corr = shrink(factor, lh, ll, mine, other)

    corr = corr[0] + swap(corr[1], "coeffici", CORE)
    corr = ring_sum(corr, "coeffici", X)
    corr = ring_sum(corr, "particle", Z)
    far0 = swap(corr, "coeffici", CORE)
    got = ring_swap([jnp.stack([corr, w[n]]) for n in (1, 2, 3)], "particle", Y)
    far = swap(jnp.stack([g[0] for g in got]), "coeffici", CORE)
    weighted = place(w, *got)
    rayleigh = assemble(corr, *got, far0, far)
    return weighted[None], rayleigh[None]


def solution(mesh):
    in_specs = (P("half", "particle", "coeffici"), P("half", "coeffici", None))
    out_specs = (P("half", ("coeffici", "particle"), None), P("half", None, None))
    return jax.shard_map(step, mesh=mesh, in_specs=in_specs, out_specs=out_specs, check_vma=False)
```

```python
import functools

import jax
import jax.numpy as jnp
from jax import lax
from jax.experimental import pallas as pl
from jax.experimental.pallas import tpu as pltpu
from jax.sharding import PartitionSpec as P


F32 = jnp.float32
BF16 = jnp.bfloat16
VMEM = pl.BlockSpec(memory_space=pltpu.VMEM)
HBM = pl.BlockSpec(memory_space=pltpu.HBM)
LANE = 128

RING = (0, 1, 3, 2)
CORE, X, Y, Z = 1, 2, 4, 1
PLACES = ((0, 3, 1, 2), (0, 1, 3, 2))


def swap(value, axis, mask):
    return lax.ppermute(value, axis, [(s, s ^ mask) for s in range(lax.axis_size(axis))])


def split(value):
    high = value.astype(BF16)
    return high, (value - high.astype(F32)).astype(BF16)


def dot(left, right):
    return lax.dot_general(left, right, (((1,), (0,)), ((), ())), preferred_element_type=F32)


def dot3(lh, ll, rh, rl):
    return dot(lh, rh) + dot(ll, rh) + dot(lh, rl)


def at(index, size):
    return pl.ds(pl.multiple_of(index * size, size), size)


def params(mib):
    return pltpu.CompilerParams(vmem_limit_bytes=mib << 20)


def shape(*dims, dtype=F32):
    return jax.ShapeDtypeStruct(dims, dtype)


def cost(flops, mib):
    return pl.CostEstimate(flops=flops, bytes_accessed=mib << 20, transcendentals=0)


def scores_kernel(side, *refs):
    if side:
        res, load, out, rh, rl, lh, ll, later, rbuf, lbuf, acc, rsems, lsems, nsems = refs
    else:
        rbuf, lh, ll, out, rh, rl, acc = refs
    me = lax.axis_index("coeffici")
    core = me & 1
    size = out.shape[1]
    depth = lh.shape[0] // 4
    copies, others = [[] for _ in range(4)], []
    if side:
        for step in range(4):
            cols = slice(step * depth, (step + 1) * depth)
            copies[step].append(pltpu.make_async_copy(load.at[cols], lbuf.at[cols], lsems.at[step]))
            for t in range(4):
                copies[step].append(
                    pltpu.make_async_copy(
                        res.at[at(2 * t + (core ^ 1), size), cols], rbuf.at[pl.ds(t * size, size), cols], rsems.at[step, t]
                    )
                )
        for t in range(4):
            others.append(
                pltpu.make_async_copy(res.at[at(2 * t + core, size)], later.at[pl.ds(t * size, size)], nsems.at[t])
            )
        for copy in copies[0] + copies[1] + copies[2]:
            copy.start()
    for step in range(4):
        for copy in copies[step]:
            copy.wait()
        for copy in (copies[3] + others[:1], others[1:], (), ())[step] if side else ():
            copy.start()
        cols = slice(step * depth, (step + 1) * depth)
        if side:
            lh[cols], ll[cols] = split(lbuf[cols])
        high, low = split(rbuf[:, cols])
        rh[:, cols], rl[:, cols] = high, low
        term = dot3(high, low, lh[cols], ll[cols])
        if step == 0:
            acc[...] = term
        else:
            acc[...] += term
    for t in range(4):
        mask = (me ^ (2 * t + (core ^ side))) >> 1
        out[mask ^ (mask >> 1)] = acc[t * size : (t + 1) * size]
    for copy in others:
        copy.wait()


def scores(side, res, *load):
    rows, coefs = res.shape
    rows = rows if side else 2 * rows
    k = load[0].shape[1]
    operand = shape(rows // 2, coefs, dtype=BF16)
    extra = (shape(coefs, k, dtype=BF16),) * 2 + (shape(rows // 2, coefs),)
    acc = pltpu.VMEM((rows // 2, k), F32)
    dma = pltpu.SemaphoreType.DMA
    return pl.pallas_call(
        functools.partial(scores_kernel, side),
        out_shape=(shape(4, rows // 8, k), operand, operand) + (extra if side else ()),
        in_specs=[HBM, HBM] if side else [VMEM] * 3,
        out_specs=(VMEM,) * (6 if side else 3),
        scratch_shapes=[pltpu.VMEM((rows // 2, coefs), F32), pltpu.VMEM((coefs, k), F32), acc, dma((4, 4)), dma((4,)), dma((4,))]
        if side
        else [acc],
        compiler_params=params(20),
        cost_estimate=cost(3 * rows * coefs * k, 6),
        name="scores_far" if side else "scores_near",
    )(res, *load)


def own_kernel(near, got, r1, r2, r3, out):
    out[...] = ((near[0] + got[0]) + (r1[...] + r2[...]) + r3[...]).T


def own_block(*terms):
    _, rows, k = terms[0].shape
    return pl.pallas_call(
        own_kernel,
        out_shape=shape(k, rows),
        in_specs=[VMEM] * 5,
        out_specs=VMEM,
        compiler_params=params(4),
        cost_estimate=cost(1 << 18, 1),
        name="own_block",
    )(*terms)


def stage_kernel(*refs):
    pieces, out = refs[:-1], refs[-1]
    me = lax.axis_index("coeffici")
    for n in range(4):
        piece = pieces[n][...] if len(pieces) == 4 else pieces[0][n]
        high, low = split(piece)
        where = at((me ^ (X * RING[n])) >> 1, LANE)
        for block in range(4):
            rows = slice(64 * block, 64 * block + 64)
            out[128 * block : 128 * block + 64, where] = high[rows]
            out[128 * block + 64 : 128 * block + 128, where] = low[rows]


def stage(*pieces):
    return pl.pallas_call(
        stage_kernel,
        out_shape=shape(4 * LANE, 4 * LANE, dtype=BF16),
        in_specs=[VMEM] * len(pieces),
        out_specs=VMEM,
        compiler_params=params(4),
        cost_estimate=cost(1 << 18, 1),
        name="stage",
    )(*pieces)


def columns(refs, ys, zs):
    return [jnp.concatenate([r[:, at(4 * y + z, LANE)] for z in zs for y in ys], axis=1) for r in refs]


def pair_kernel(places, sides, add, *refs):
    ops, before, (out_p, out_q) = refs[: 3 * sides], refs[3 * sides : 3 * sides + 2 * add], refs[-2:]
    particle = lax.axis_index("particle")
    y, z = particle >> 2, particle & 3
    starts = [(y ^ PLACES[part][place]) * LANE + 32 * part for part in range(2) for place in places]
    starts += [s + 64 for s in starts]
    wide = out_p.shape[2]

    @pl.loop(0, 2)
    def _(step):
        spots = [2 * step, 2 * step + 1]
        total = None
        for side in range(sides):
            st, rh, rl = ops[3 * side : 3 * side + 3]
            high, rest = columns((rh, rl), range(3), [z ^ s ^ (s >> 1) for s in spots])
            left = jnp.concatenate([st[pl.ds(pl.multiple_of(s, 32), 32)] for s in starts])
            both, low = dot(left, high), dot(left[:LANE], rest)
            term = both[:LANE] + both[LANE:] + low
            total = term if total is None else total + term
        for part, out in enumerate((out_p, out_q)):
            for n in range(2):
                for i, spot in enumerate(spots):
                    top = 64 * part + 32 * n
                    value = total[top : top + 32, wide * i : wide * (i + 1)]
                    if add:
                        value = value + before[part][4 * n + spot]
                    out[4 * n + spot] = value


def covariance_pair(places, operands, before):
    rows, coefs = operands[1].shape
    sides = len(operands) // 3
    out = shape(8, 32, 3 * LANE)
    return pl.pallas_call(
        functools.partial(pair_kernel, places, sides, len(before) // 2),
        out_shape=(out, out),
        in_specs=[VMEM] * (len(operands) + len(before)),
        out_specs=(VMEM, VMEM),
        compiler_params=params(16),
        cost_estimate=cost(3 * rows * coefs * LANE * sides, 4),
    )(*operands, *before)


def third_kernel(*refs):
    ops, out = refs[:6], refs[6]
    particle = lax.axis_index("particle")
    y, z = particle >> 2, particle & 3

    @pl.loop(0, 2)
    def _(step):
        spots = [2 * step, 2 * step + 1]
        both = low = None
        for st, rh, rl in (ops[:3], ops[3:]):
            high, rest = columns((rh, rl), [3], [z ^ s ^ (s >> 1) for s in spots])
            left_high = jnp.concatenate([st[LANE * b : LANE * b + 64] for b in range(4)])
            first, second = dot(st[...], high), dot(left_high, rest)
            both = first if both is None else both + first
            low = second if low is None else low + second
        for b in range(4):
            mask = y ^ b
            place = mask ^ (mask >> 1)
            top = LANE * b
            value = both[top : top + 64] + both[top + 64 : top + LANE] + low[64 * b : 64 * b + 64]
            for i, spot in enumerate(spots):
                out[4 * spot + place] = value[:, LANE * i : LANE * (i + 1)]


def covariance_third(operands):
    rows, coefs = operands[1].shape
    return pl.pallas_call(
        third_kernel,
        out_shape=shape(16, 64, LANE),
        in_specs=[VMEM] * 6,
        out_specs=VMEM,
        compiler_params=params(16),
        cost_estimate=cost(3 * rows * coefs * LANE, 4),
        name="covariance_third",
    )(*operands)


def shrink_kernel(factor, load_h, load_l, mine, other, w_out, corr_out, cbuf):
    particle = lax.axis_index("particle")
    y, z = particle >> 2, particle & 3
    core = lax.axis_index("coeffici") & 1
    corr = None
    for n in range(4):
        cols = slice(n * LANE, n * LANE + LANE)
        cov = mine[:, cols] * factor
        far = other[:, cols] * factor
        weighted = cov * jax.nn.sigmoid(cov * far)
        mask = y ^ n
        w_out[mask ^ (mask >> 1)] = weighted
        wh, wl = split(weighted)
        where = at(4 * n + z, LANE)
        term = dot3(wh, wl, load_h[where], load_l[where])
        corr = term if corr is None else corr + term
    cbuf[...] = corr * factor
    for n in range(2):
        rows = cbuf[at(core ^ n, 32)]
        corr_out[n, :32] = rows[:, :LANE]
        corr_out[n, 32:] = rows[:, LANE:]


def shrink(factor, *args):
    return pl.pallas_call(
        functools.partial(shrink_kernel, factor),
        out_shape=(shape(4, 64, LANE), shape(2, 64, LANE)),
        in_specs=[VMEM] * 4,
        out_specs=(VMEM, VMEM),
        scratch_shapes=[pltpu.VMEM((64, 2 * LANE), F32)],
        compiler_params=params(8),
        cost_estimate=cost(6 * 64 * 512 * 256, 1),
        name="shrink",
    )(*args)


def place_kernel(w, r1, r2, r3, out, buf):
    y = lax.axis_index("particle") >> 2
    for mask, piece in zip(RING, (w[0], r1[1], r2[1], r3[1])):
        buf[at(y ^ mask, 64)] = piece
    out[...] = buf[...].T


def assemble_kernel(near0, r1, r2, r3, far0, far, out, buf):
    y = lax.axis_index("particle") >> 2
    core = lax.axis_index("coeffici") & 1
    near = (near0[...], r1[0], r2[0], r3[0])
    for n in range(4):
        for c, piece in enumerate((near[n], far0[...] if n == 0 else far[n - 1])):
            where = at(2 * (y ^ RING[n]) + (core ^ c), 32)
            buf[where, :LANE] = piece[:32]
            buf[where, LANE:] = piece[32:]
    out[...] = buf[...].T


def place(*args):
    return pl.pallas_call(
        place_kernel,
        out_shape=shape(LANE, 2 * LANE),
        in_specs=[VMEM] * len(args),
        out_specs=VMEM,
        scratch_shapes=[pltpu.VMEM((2 * LANE, LANE), F32)],
        compiler_params=params(4),
        cost_estimate=cost(1 << 18, 1),
        name="place",
    )(*args)


def assemble(*args):
    k = 2 * LANE
    return pl.pallas_call(
        assemble_kernel,
        out_shape=shape(k, k),
        in_specs=[VMEM] * len(args),
        out_specs=VMEM,
        scratch_shapes=[pltpu.VMEM((k, k), F32)],
        compiler_params=params(4),
        name="assemble",
    )(*args)


def ring_swap(values, axis, unit):
    swapped = []
    for v, m in zip(values, RING[1:]):
        swapped.append(swap(v, axis, unit * m))
    return swapped


def ring_sum(value, axis, unit):
    a, b, c = ring_swap([value] * 3, axis, unit)
    return (value + a) + (b + c)


def step(residuals, loadings):
    res, load = (pltpu.with_memory_space_constraint(v[0], pltpu.HBM) for v in (residuals, loadings))
    factor = (res.shape[0] * lax.axis_size("particle")) ** -0.5

    far, fh, fl, lh, ll, rest = scores(1, res, load)
    got = swap(far, "coeffici", CORE)
    near, nh, nl = scores(0, rest, lh, ll)
    own = own_block(near, got, *ring_swap([near[n] + got[n] for n in (1, 2, 3)], "coeffici", X))
    pieces = [own] + ring_swap([own] * 3, "coeffici", X)
    others = swap(jnp.stack(pieces), "coeffici", CORE)
    near_ops = (stage(*pieces), nh, nl)
    far_ops = (stage(others), fh, fl)

    leave = covariance_pair((2, 3), near_ops, ())
    leave_p, leave_q = covariance_pair((2, 3), far_ops, leave)
    one_p = swap(leave_p, "particle", Y)
    one_q = swap(leave_q, "particle", 3 * Y)
    third = covariance_third(near_ops + far_ops)
    sums = ring_swap([third[4 * n : 4 * n + 4] for n in (1, 2, 3)], "particle", Z)
    keep_p, keep_q = covariance_pair((0, 1), near_ops + far_ops, ())
    two_p = swap(keep_p[4:] + one_p[4:], "particle", 3 * Y)
    two_q = swap(keep_q[4:] + one_q[4:], "particle", Y)

    def at_z(n):
        return jnp.concatenate([keep_p[n] + one_p[n] + two_p[n], keep_q[n] + one_q[n] + two_q[n]])

    def at_y(n):
        return third[n] + (sums[0][n] + sums[1][n]) + sums[2][n]

    r1, r2, r3 = ring_swap([at_z(n) for n in (1, 2, 3)], "particle", Z)
    t1, t2, t3 = ring_swap([at_y(n) for n in (1, 2, 3)], "particle", Y)
    mine = jnp.concatenate([at_z(0) + (r1 + r2) + r3, at_y(0) + (t1 + t2) + t3], axis=1)
    other = swap(mine, "half", 1)
    w, corr = shrink(factor, lh, ll, mine, other)

    corr = corr[0] + swap(corr[1], "coeffici", CORE)
    corr = ring_sum(corr, "coeffici", X)
    corr = ring_sum(corr, "particle", Z)
    far0 = swap(corr, "coeffici", CORE)
    got = ring_swap([jnp.stack([corr, w[n]]) for n in (1, 2, 3)], "particle", Y)
    far = swap(jnp.stack([g[0] for g in got]), "coeffici", CORE)
    weighted = place(w, *got)
    rayleigh = assemble(corr, *got, far0, far)
    return weighted[None], rayleigh[None]


def solution(mesh):
    in_specs = (P("half", "particle", "coeffici"), P("half", "coeffici", None))
    out_specs = (P("half", ("coeffici", "particle"), None), P("half", None, None))
    return jax.shard_map(step, mesh=mesh, in_specs=in_specs, out_specs=out_specs, check_vma=False)
```

```python
import functools

import jax
import jax.numpy as jnp
from jax import lax
from jax.experimental import pallas as pl
from jax.experimental.pallas import tpu as pltpu
from jax.sharding import PartitionSpec as P


F32 = jnp.float32
BF16 = jnp.bfloat16
VMEM = pl.BlockSpec(memory_space=pltpu.VMEM)
HBM = pl.BlockSpec(memory_space=pltpu.HBM)
LANE = 128

RING = (0, 1, 3, 2)
CORE, X, Y, Z = 1, 2, 4, 1
PLACES = ((0, 3, 1, 2), (0, 1, 3, 2))


def swap(value, axis, mask):
    return lax.ppermute(value, axis, [(s, s ^ mask) for s in range(lax.axis_size(axis))])


def split(value):
    high = value.astype(BF16)
    return high, (value - high.astype(F32)).astype(BF16)


def dot(left, right):
    return lax.dot_general(left, right, (((1,), (0,)), ((), ())), preferred_element_type=F32)


def dot3(lh, ll, rh, rl):
    return dot(lh, rh) + dot(ll, rh) + dot(lh, rl)


def at(index, size):
    return pl.ds(pl.multiple_of(index * size, size), size)


def params(mib):
    return pltpu.CompilerParams(vmem_limit_bytes=mib << 20)


def shape(*dims, dtype=F32):
    return jax.ShapeDtypeStruct(dims, dtype)


def cost(flops, mib):
    return pl.CostEstimate(flops=flops, bytes_accessed=mib << 20, transcendentals=0)


TURNS = ((1, (1, 2)), (0, (1, 2)), (1, (3, 0)), (0, (3, 0)))


def scores_kernel(turn, *refs):
    last = turn == len(TURNS) - 1
    if turn == 0:
        res, load, out, rh, rl, lh, ll, later, rbuf, lbuf, acc, nsems, rsems, lsems = refs
    elif last:
        rbuf, lh, ll, out, rh, rl, acc = refs
    else:
        rbuf, lh, ll, res, out, rh, rl, later, acc, nsems = refs
    me = lax.axis_index("coeffici")
    size = out.shape[1]
    depth = lh.shape[0] // 4

    def rows_of(turn, n):
        side, places = TURNS[turn]
        return at(me ^ side ^ (X * RING[places[n]]), size)

    copies, others = [[] for _ in range(4)], []
    if not last:
        for n in range(2):
            others.append(
                pltpu.make_async_copy(res.at[rows_of(turn + 1, n)], later.at[pl.ds(n * size, size)], nsems.at[n])
            )
    if turn == 0:
        for step in range(4):
            cols = slice(step * depth, (step + 1) * depth)
            copies[step].append(pltpu.make_async_copy(load.at[cols], lbuf.at[cols], lsems.at[step]))
            for n in range(2):
                copies[step].append(
                    pltpu.make_async_copy(
                        res.at[rows_of(0, n), cols], rbuf.at[pl.ds(n * size, size), cols], rsems.at[step, n]
                    )
                )
        for copy in copies[0] + copies[1]:
            copy.start()
    else:
        for copy in others:
            copy.start()
    for step in range(4):
        for copy in copies[step]:
            copy.wait()
        for copy in (copies[2], copies[3], others, ())[step] if turn == 0 else ():
            copy.start()
        cols = slice(step * depth, (step + 1) * depth)
        if turn == 0:
            lh[cols], ll[cols] = split(lbuf[cols])
        high, low = split(rbuf[:, cols])
        rh[:, cols], rl[:, cols] = high, low
        term = dot3(high, low, lh[cols], ll[cols])
        if step == 0:
            acc[...] = term
        else:
            acc[...] += term
    for n in range(2):
        out[n] = acc[n * size : (n + 1) * size]
    for copy in others:
        copy.wait()


def scores(turn, coefs, k, size, *args):
    last = turn == len(TURNS) - 1
    operand = shape(2 * size, coefs, dtype=BF16)
    loads = (shape(coefs, k, dtype=BF16),) * 2 if turn == 0 else ()
    dma = pltpu.SemaphoreType.DMA
    scratch = [pltpu.VMEM((2 * size, k), F32)] + ([] if last else [dma((2,))])
    if turn == 0:
        scratch = [pltpu.VMEM((2 * size, coefs), F32), pltpu.VMEM((coefs, k), F32)] + scratch + [dma((4, 2)), dma((4,))]
    outs = (shape(2, size, k), operand, operand) + loads + (() if last else (shape(2 * size, coefs),))
    return pl.pallas_call(
        functools.partial(scores_kernel, turn),
        out_shape=outs,
        in_specs=[HBM, HBM] if turn == 0 else [VMEM] * 3 + ([] if last else [HBM]),
        out_specs=(VMEM,) * len(outs),
        scratch_shapes=scratch,
        compiler_params=params(16),
        cost_estimate=cost(12 * size * coefs * k, 4),
    )(*args)


def own_kernel(near, got, r1, r2, r3, out):
    out[...] = ((near[1] + got[1]) + (r1[...] + r2[...]) + r3[...]).T


def own_block(*terms):
    _, rows, k = terms[0].shape
    return pl.pallas_call(
        own_kernel,
        out_shape=shape(k, rows),
        in_specs=[VMEM] * 5,
        out_specs=VMEM,
        compiler_params=params(4),
        cost_estimate=cost(1 << 18, 1),
        name="own_block",
    )(*terms)


def stage_kernel(*refs):
    pieces, outs = refs[:-2], refs[-2:]
    for out, places in zip(outs, ((1, 2), (3, 0))):
        for n, spot in enumerate(places):
            high, low = split(pieces[spot][...] if len(pieces) == 4 else pieces[0][spot])
            where = slice(n * LANE, (n + 1) * LANE)
            for block in range(4):
                rows = slice(64 * block, 64 * block + 64)
                out[128 * block : 128 * block + 64, where] = high[rows]
                out[128 * block + 64 : 128 * block + 128, where] = low[rows]


def stage(*pieces):
    out = shape(4 * LANE, 2 * LANE, dtype=BF16)
    return pl.pallas_call(
        stage_kernel,
        out_shape=(out, out),
        in_specs=[VMEM] * len(pieces),
        out_specs=(VMEM, VMEM),
        compiler_params=params(4),
        cost_estimate=cost(1 << 18, 1),
        name="stage",
    )(*pieces)


def columns(refs, ys, zs):
    return [jnp.concatenate([r[:, at(4 * y + z, LANE)] for z in zs for y in ys], axis=1) for r in refs]


def pair_kernel(places, sides, add, *refs):
    ops, before, (out_p, out_q) = refs[: 3 * sides], refs[3 * sides : 3 * sides + 2 * add], refs[-2:]
    particle = lax.axis_index("particle")
    y, z = particle >> 2, particle & 3
    starts = [(y ^ PLACES[part][place]) * LANE + 32 * part for part in range(2) for place in places]
    starts += [s + 64 for s in starts]
    wide = out_p.shape[2]

    @pl.loop(0, 2)
    def _(step):
        spots = [2 * step, 2 * step + 1]
        total = None
        for side in range(sides):
            st, rh, rl = ops[3 * side : 3 * side + 3]
            high, rest = columns((rh, rl), range(3), [z ^ s ^ (s >> 1) for s in spots])
            left = jnp.concatenate([st[pl.ds(pl.multiple_of(s, 32), 32)] for s in starts])
            both, low = dot(left, high), dot(left[:LANE], rest)
            term = both[:LANE] + both[LANE:] + low
            total = term if total is None else total + term
        for part, out in enumerate((out_p, out_q)):
            for n in range(2):
                for i, spot in enumerate(spots):
                    top = 64 * part + 32 * n
                    value = total[top : top + 32, wide * i : wide * (i + 1)]
                    if add:
                        value = value + before[part][4 * n + spot]
                    out[4 * n + spot] = value


def covariance_pair(places, operands, before):
    rows, coefs = operands[1].shape
    sides = len(operands) // 3
    out = shape(8, 32, 3 * LANE)
    return pl.pallas_call(
        functools.partial(pair_kernel, places, sides, len(before) // 2),
        out_shape=(out, out),
        in_specs=[VMEM] * (len(operands) + len(before)),
        out_specs=(VMEM, VMEM),
        compiler_params=params(16),
        cost_estimate=cost(3 * rows * coefs * LANE * sides, 4),
    )(*operands, *before)


def third_kernel(*refs):
    ops, out = refs[:-1], refs[-1]
    particle = lax.axis_index("particle")
    y, z = particle >> 2, particle & 3

    @pl.loop(0, 2)
    def _(step):
        spots = [2 * step, 2 * step + 1]
        both = low = None
        for side in range(len(ops) // 3):
            st, rh, rl = ops[3 * side : 3 * side + 3]
            high, rest = columns((rh, rl), [3], [z ^ s ^ (s >> 1) for s in spots])
            left_high = jnp.concatenate([st[LANE * b : LANE * b + 64] for b in range(4)])
            first, second = dot(st[...], high), dot(left_high, rest)
            both = first if both is None else both + first
            low = second if low is None else low + second
        for b in range(4):
            mask = y ^ b
            place = mask ^ (mask >> 1)
            top = LANE * b
            value = both[top : top + 64] + both[top + 64 : top + LANE] + low[64 * b : 64 * b + 64]
            for i, spot in enumerate(spots):
                out[4 * spot + place] = value[:, LANE * i : LANE * (i + 1)]


def covariance_third(operands):
    rows, coefs = operands[1].shape
    return pl.pallas_call(
        third_kernel,
        out_shape=shape(16, 64, LANE),
        in_specs=[VMEM] * len(operands),
        out_specs=VMEM,
        compiler_params=params(16),
        cost_estimate=cost(6 * rows * coefs * LANE, 4),
        name="covariance_third",
    )(*operands)


def shrink_kernel(factor, load_h, load_l, mine, other, w_out, corr_out, cbuf):
    particle = lax.axis_index("particle")
    y, z = particle >> 2, particle & 3
    core = lax.axis_index("coeffici") & 1
    corr = None
    for n in range(4):
        cols = slice(n * LANE, n * LANE + LANE)
        cov = mine[:, cols] * factor
        far = other[:, cols] * factor
        weighted = cov * jax.nn.sigmoid(cov * far)
        mask = y ^ n
        w_out[mask ^ (mask >> 1)] = weighted
        wh, wl = split(weighted)
        where = at(4 * n + z, LANE)
        term = dot3(wh, wl, load_h[where], load_l[where])
        corr = term if corr is None else corr + term
    cbuf[...] = corr * factor
    for n in range(2):
        rows = cbuf[at(core ^ n, 32)]
        corr_out[n, :32] = rows[:, :LANE]
        corr_out[n, 32:] = rows[:, LANE:]


def shrink(factor, *args):
    return pl.pallas_call(
        functools.partial(shrink_kernel, factor),
        out_shape=(shape(4, 64, LANE), shape(2, 64, LANE)),
        in_specs=[VMEM] * 4,
        out_specs=(VMEM, VMEM),
        scratch_shapes=[pltpu.VMEM((64, 2 * LANE), F32)],
        compiler_params=params(8),
        cost_estimate=cost(6 * 64 * 512 * 256, 1),
        name="shrink",
    )(*args)


def place_kernel(w, r1, r2, r3, out, buf):
    y = lax.axis_index("particle") >> 2
    for mask, piece in zip(RING, (w[0], r1[1], r2[1], r3[1])):
        buf[at(y ^ mask, 64)] = piece
    out[...] = buf[...].T


def assemble_kernel(near0, r1, r2, r3, far0, far, out, buf):
    y = lax.axis_index("particle") >> 2
    core = lax.axis_index("coeffici") & 1
    near = (near0[...], r1[0], r2[0], r3[0])
    for n in range(4):
        for c, piece in enumerate((near[n], far0[...] if n == 0 else far[n - 1])):
            where = at(2 * (y ^ RING[n]) + (core ^ c), 32)
            buf[where, :LANE] = piece[:32]
            buf[where, LANE:] = piece[32:]
    out[...] = buf[...].T


def place(*args):
    return pl.pallas_call(
        place_kernel,
        out_shape=shape(LANE, 2 * LANE),
        in_specs=[VMEM] * len(args),
        out_specs=VMEM,
        scratch_shapes=[pltpu.VMEM((2 * LANE, LANE), F32)],
        compiler_params=params(4),
        cost_estimate=cost(1 << 18, 1),
        name="place",
    )(*args)


def assemble(*args):
    k = 2 * LANE
    return pl.pallas_call(
        assemble_kernel,
        out_shape=shape(k, k),
        in_specs=[VMEM] * len(args),
        out_specs=VMEM,
        scratch_shapes=[pltpu.VMEM((k, k), F32)],
        compiler_params=params(4),
        name="assemble",
    )(*args)


def ring_swap(values, axis, unit):
    return [swap(v, axis, unit * m) for v, m in zip(values, RING[1:])]


def ring_sum(value, axis, unit):
    a, b, c = ring_swap([value] * 3, axis, unit)
    return (value + a) + (b + c)


def step(residuals, loadings):
    res, load = (pltpu.with_memory_space_constraint(v[0], pltpu.HBM) for v in (residuals, loadings))
    factor = (res.shape[0] * lax.axis_size("particle")) ** -0.5

    sizes = (res.shape[1], load.shape[1], res.shape[0] // 8)
    far_a, fh_a, fl_a, lh, ll, rest = scores(0, *sizes, res, load)
    got_a = swap(far_a, "coeffici", CORE)
    near_a, nh_a, nl_a, rest = scores(1, *sizes, rest, lh, ll, res)
    r1 = swap(near_a[0] + got_a[0], "coeffici", X * RING[1])
    r2 = swap(near_a[1] + got_a[1], "coeffici", X * RING[2])
    far_b, fh_b, fl_b, rest = scores(2, *sizes, rest, lh, ll, res)
    got_b = swap(far_b, "coeffici", CORE)
    near_b, nh_b, nl_b = scores(3, *sizes, rest, lh, ll)
    r3 = swap(near_b[0] + got_b[0], "coeffici", X * RING[3])
    own = own_block(near_b, got_b, r1, r2, r3)
    pieces = [own] + ring_swap([own] * 3, "coeffici", X)
    others = swap(jnp.stack(pieces), "coeffici", CORE)
    st_a, st_b = stage(*pieces)
    near_ops = (st_a, nh_a, nl_a, st_b, nh_b, nl_b)
    st_a, st_b = stage(others)
    far_ops = (st_a, fh_a, fl_a, st_b, fh_b, fl_b)

    leave = covariance_pair((2, 3), near_ops, ())
    leave_p, leave_q = covariance_pair((2, 3), far_ops, leave)
    one_p = swap(leave_p, "particle", Y)
    one_q = swap(leave_q, "particle", 3 * Y)
    third = covariance_third(near_ops + far_ops)
    sums = ring_swap([third[4 * n : 4 * n + 4] for n in (1, 2, 3)], "particle", Z)
    keep_p, keep_q = covariance_pair((0, 1), near_ops + far_ops, ())
    two_p = swap(keep_p[4:] + one_p[4:], "particle", 3 * Y)
    two_q = swap(keep_q[4:] + one_q[4:], "particle", Y)

    def at_z(n):
        return jnp.concatenate([keep_p[n] + one_p[n] + two_p[n], keep_q[n] + one_q[n] + two_q[n]])

    def at_y(n):
        return third[n] + (sums[0][n] + sums[1][n]) + sums[2][n]

    r1, r2, r3 = ring_swap([at_z(n) for n in (1, 2, 3)], "particle", Z)
    t1, t2, t3 = ring_swap([at_y(n) for n in (1, 2, 3)], "particle", Y)
    mine = jnp.concatenate([at_z(0) + (r1 + r2) + r3, at_y(0) + (t1 + t2) + t3], axis=1)
    other = swap(mine, "half", 1)
    w, corr = shrink(factor, lh, ll, mine, other)

    corr = corr[0] + swap(corr[1], "coeffici", CORE)
    corr = ring_sum(corr, "coeffici", X)
    corr = ring_sum(corr, "particle", Z)
    far0 = swap(corr, "coeffici", CORE)
    got = ring_swap([jnp.stack([corr, w[n]]) for n in (1, 2, 3)], "particle", Y)
    far = swap(jnp.stack([g[0] for g in got]), "coeffici", CORE)
    weighted = place(w, *got)
    rayleigh = assemble(corr, *got, far0, far)
    return weighted[None], rayleigh[None]


def solution(mesh):
    in_specs = (P("half", "particle", "coeffici"), P("half", "coeffici", None))
    out_specs = (P("half", ("coeffici", "particle"), None), P("half", None, None))
    return jax.shard_map(step, mesh=mesh, in_specs=in_specs, out_specs=out_specs, check_vma=False)
```

```python
import functools

import jax
import jax.numpy as jnp
from jax import lax
from jax.experimental import pallas as pl
from jax.experimental.pallas import tpu as pltpu
from jax.sharding import PartitionSpec as P


F32 = jnp.float32
BF16 = jnp.bfloat16
VMEM = pl.BlockSpec(memory_space=pltpu.VMEM)
HBM = pl.BlockSpec(memory_space=pltpu.HBM)
LANE = 128

RING = (0, 1, 3, 2)
CORE, X, Y, Z = 1, 2, 4, 1
PLACES = ((0, 3, 1, 2), (0, 1, 3, 2))


def swap(value, axis, mask):
    return lax.ppermute(value, axis, [(s, s ^ mask) for s in range(lax.axis_size(axis))])


def split(value):
    high = value.astype(BF16)
    return high, (value - high.astype(F32)).astype(BF16)


def dot(left, right):
    return lax.dot_general(left, right, (((1,), (0,)), ((), ())), preferred_element_type=F32)


def dot3(lh, ll, rh, rl):
    return dot(lh, rh) + dot(ll, rh) + dot(lh, rl)


def at(index, size):
    return pl.ds(pl.multiple_of(index * size, size), size)


def params(mib):
    return pltpu.CompilerParams(vmem_limit_bytes=mib << 20)


def shape(*dims, dtype=F32):
    return jax.ShapeDtypeStruct(dims, dtype)


def cost(flops, mib):
    return pl.CostEstimate(flops=flops, bytes_accessed=mib << 20, transcendentals=0)


def scores_kernel(side, *refs):
    if side:
        res, load, out, rh, rl, lh, ll, later, rbuf, lbuf, acc, rsems, lsems, nsems = refs
    else:
        rbuf, lh, ll, out, rh, rl, acc = refs
    me = lax.axis_index("coeffici")
    size = out.shape[1]
    depth = lh.shape[0] // 4
    copies, others = [[] for _ in range(4)], []
    if side:
        for step in range(4):
            cols = slice(step * depth, (step + 1) * depth)
            copies[step].append(pltpu.make_async_copy(load.at[cols], lbuf.at[cols], lsems.at[step]))
            for t in range(4):
                copies[step].append(
                    pltpu.make_async_copy(
                        res.at[at(me ^ 1 ^ (X * RING[t]), size), cols], rbuf.at[pl.ds(t * size, size), cols], rsems.at[step, t]
                    )
                )
        for t in range(4):
            others.append(
                pltpu.make_async_copy(res.at[at(me ^ (X * RING[t]), size)], later.at[pl.ds(t * size, size)], nsems.at[t])
            )
        for copy in copies[0] + copies[1]:
            copy.start()
    for step in range(4):
        for copy in copies[step]:
            copy.wait()
        for copy in (copies[2], copies[3] + others[:1], others[1:], ())[step] if side else ():
            copy.start()
        cols = slice(step * depth, (step + 1) * depth)
        if side:
            lh[cols], ll[cols] = split(lbuf[cols])
        high, low = split(rbuf[:, cols])
        rh[:, cols], rl[:, cols] = high, low
        term = dot3(high, low, lh[cols], ll[cols])
        if step == 0:
            acc[...] = term
        else:
            acc[...] += term
    for t in range(4):
        out[t] = acc[t * size : (t + 1) * size]
    for copy in others:
        copy.wait()


def scores(side, res, *load):
    rows, coefs = res.shape
    rows = rows if side else 2 * rows
    k = load[0].shape[1]
    operand = shape(rows // 2, coefs, dtype=BF16)
    extra = (shape(coefs, k, dtype=BF16),) * 2 + (shape(rows // 2, coefs),)
    acc = pltpu.VMEM((rows // 2, k), F32)
    dma = pltpu.SemaphoreType.DMA
    return pl.pallas_call(
        functools.partial(scores_kernel, side),
        out_shape=(shape(4, rows // 8, k), operand, operand) + (extra if side else ()),
        in_specs=[HBM, HBM] if side else [VMEM] * 3,
        out_specs=(VMEM,) * (6 if side else 3),
        scratch_shapes=[pltpu.VMEM((rows // 2, coefs), F32), pltpu.VMEM((coefs, k), F32), acc, dma((4, 4)), dma((4,)), dma((4,))]
        if side
        else [acc],
        compiler_params=params(20),
        cost_estimate=cost(3 * rows * coefs * k, 6),
        name="scores_far" if side else "scores_near",
    )(res, *load)


def own_kernel(near, got, r1, r2, r3, out):
    out[...] = ((near[0] + got[0]) + (r1[...] + r2[...]) + r3[...]).T


def own_block(*terms):
    _, rows, k = terms[0].shape
    return pl.pallas_call(
        own_kernel,
        out_shape=shape(k, rows),
        in_specs=[VMEM] * 5,
        out_specs=VMEM,
        compiler_params=params(4),
        cost_estimate=cost(1 << 18, 1),
        name="own_block",
    )(*terms)


def stage_kernel(*refs):
    pieces, out = refs[:-1], refs[-1]
    for n in range(2):
        high, low = split(pieces[n][...] if len(pieces) == 2 else pieces[0][n])
        where = slice(n * LANE, (n + 1) * LANE)
        for block in range(4):
            rows = slice(64 * block, 64 * block + 64)
            out[128 * block : 128 * block + 64, where] = high[rows]
            out[128 * block + 64 : 128 * block + 128, where] = low[rows]


def stage(*pieces):
    return pl.pallas_call(
        stage_kernel,
        out_shape=shape(4 * LANE, 2 * LANE, dtype=BF16),
        in_specs=[VMEM] * len(pieces),
        out_specs=VMEM,
        compiler_params=params(4),
        cost_estimate=cost(1 << 18, 1),
        name="stage",
    )(*pieces)


def columns(refs, half, ys, zs):
    rows = slice(2 * LANE * half, 2 * LANE * (half + 1))
    return [jnp.concatenate([r[rows, at(4 * y + z, LANE)] for z in zs for y in ys], axis=1) for r in refs]


def pair_kernel(places, half, sides, add, *refs):
    ops, before, (out_p, out_q) = refs[: 3 * sides], refs[3 * sides : 3 * sides + 2 * add], refs[-2:]
    particle = lax.axis_index("particle")
    y, z = particle >> 2, particle & 3
    starts = [(y ^ PLACES[part][place]) * LANE + 32 * part for part in range(2) for place in places]
    starts += [s + 64 for s in starts]
    wide = out_p.shape[2]

    @pl.loop(0, 2)
    def _(step):
        spots = [2 * step, 2 * step + 1]
        total = None
        for side in range(sides):
            st, rh, rl = ops[3 * side : 3 * side + 3]
            high, rest = columns((rh, rl), half, range(3), [z ^ s ^ (s >> 1) for s in spots])
            left = jnp.concatenate([st[pl.ds(pl.multiple_of(s, 32), 32)] for s in starts])
            both, low = dot(left, high), dot(left[:LANE], rest)
            term = both[:LANE] + both[LANE:] + low
            total = term if total is None else total + term
        for part, out in enumerate((out_p, out_q)):
            for n in range(2):
                for i, spot in enumerate(spots):
                    top = 64 * part + 32 * n
                    value = total[top : top + 32, wide * i : wide * (i + 1)]
                    if add:
                        value = value + before[part][4 * n + spot]
                    out[4 * n + spot] = value


def covariance_pair(places, half, operands, before):
    rows, coefs = operands[1].shape
    sides = len(operands) // 3
    out = shape(8, 32, 3 * LANE)
    return pl.pallas_call(
        functools.partial(pair_kernel, places, half, sides, len(before) // 2),
        out_shape=(out, out),
        in_specs=[VMEM] * (len(operands) + len(before)),
        out_specs=(VMEM, VMEM),
        compiler_params=params(16),
        cost_estimate=cost(2 * rows * coefs * LANE * sides, 4),
    )(*operands, *before)


def third_kernel(half, *refs):
    ops, before, out = refs[:6], refs[6:-1], refs[-1]
    particle = lax.axis_index("particle")
    y, z = particle >> 2, particle & 3

    @pl.loop(0, 2)
    def _(step):
        spots = [2 * step, 2 * step + 1]
        both = low = None
        for st, rh, rl in (ops[:3], ops[3:]):
            high, rest = columns((rh, rl), half, [3], [z ^ s ^ (s >> 1) for s in spots])
            left_high = jnp.concatenate([st[LANE * b : LANE * b + 64] for b in range(4)])
            first, second = dot(st[...], high), dot(left_high, rest)
            both = first if both is None else both + first
            low = second if low is None else low + second
        for b in range(4):
            mask = y ^ b
            place = mask ^ (mask >> 1)
            top = LANE * b
            value = both[top : top + 64] + both[top + 64 : top + LANE] + low[64 * b : 64 * b + 64]
            for i, spot in enumerate(spots):
                mine = value[:, LANE * i : LANE * (i + 1)]
                out[4 * spot + place] = mine + before[0][4 * spot + place] if before else mine


def covariance_third(half, operands, *before):
    rows, coefs = operands[1].shape
    return pl.pallas_call(
        functools.partial(third_kernel, half),
        out_shape=shape(16, 64, LANE),
        in_specs=[VMEM] * (6 + len(before)),
        out_specs=VMEM,
        compiler_params=params(16),
        cost_estimate=cost(3 * rows * coefs * LANE, 4),
        name="covariance_third",
    )(*operands, *before)


def shrink_kernel(factor, load_h, load_l, mine, other, w_out, corr_out, cbuf):
    particle = lax.axis_index("particle")
    y, z = particle >> 2, particle & 3
    core = lax.axis_index("coeffici") & 1
    corr = None
    for n in range(4):
        cols = slice(n * LANE, n * LANE + LANE)
        cov = mine[:, cols] * factor
        far = other[:, cols] * factor
        weighted = cov * jax.nn.sigmoid(cov * far)
        mask = y ^ n
        w_out[mask ^ (mask >> 1)] = weighted
        wh, wl = split(weighted)
        where = at(4 * n + z, LANE)
        term = dot3(wh, wl, load_h[where], load_l[where])
        corr = term if corr is None else corr + term
    cbuf[...] = corr * factor
    for n in range(2):
        rows = cbuf[at(core ^ n, 32)]
        corr_out[n, :32] = rows[:, :LANE]
        corr_out[n, 32:] = rows[:, LANE:]


def shrink(factor, *args):
    return pl.pallas_call(
        functools.partial(shrink_kernel, factor),
        out_shape=(shape(4, 64, LANE), shape(2, 64, LANE)),
        in_specs=[VMEM] * 4,
        out_specs=(VMEM, VMEM),
        scratch_shapes=[pltpu.VMEM((64, 2 * LANE), F32)],
        compiler_params=params(8),
        cost_estimate=cost(6 * 64 * 512 * 256, 1),
        name="shrink",
    )(*args)


def place_kernel(w, r1, r2, r3, out, buf):
    y = lax.axis_index("particle") >> 2
    for mask, piece in zip(RING, (w[0], r1[1], r2[1], r3[1])):
        buf[at(y ^ mask, 64)] = piece
    out[...] = buf[...].T


def assemble_kernel(near0, r1, r2, r3, far0, far, out, buf):
    y = lax.axis_index("particle") >> 2
    core = lax.axis_index("coeffici") & 1
    near = (near0[...], r1[0], r2[0], r3[0])
    for n in range(4):
        for c, piece in enumerate((near[n], far0[...] if n == 0 else far[n - 1])):
            where = at(2 * (y ^ RING[n]) + (core ^ c), 32)
            buf[where, :LANE] = piece[:32]
            buf[where, LANE:] = piece[32:]
    out[...] = buf[...].T


def place(*args):
    return pl.pallas_call(
        place_kernel,
        out_shape=shape(LANE, 2 * LANE),
        in_specs=[VMEM] * len(args),
        out_specs=VMEM,
        scratch_shapes=[pltpu.VMEM((2 * LANE, LANE), F32)],
        compiler_params=params(4),
        cost_estimate=cost(1 << 18, 1),
        name="place",
    )(*args)


def assemble(*args):
    k = 2 * LANE
    return pl.pallas_call(
        assemble_kernel,
        out_shape=shape(k, k),
        in_specs=[VMEM] * len(args),
        out_specs=VMEM,
        scratch_shapes=[pltpu.VMEM((k, k), F32)],
        compiler_params=params(4),
        name="assemble",
    )(*args)


def ring_swap(values, axis, unit):
    swapped = []
    for v, m in zip(values, RING[1:]):
        swapped.append(swap(v, axis, unit * m))
    return swapped


def ring_sum(value, axis, unit):
    a, b, c = ring_swap([value] * 3, axis, unit)
    return (value + a) + (b + c)


def step(residuals, loadings):
    res, load = (pltpu.with_memory_space_constraint(v[0], pltpu.HBM) for v in (residuals, loadings))
    factor = (res.shape[0] * lax.axis_size("particle")) ** -0.5

    far, fh, fl, lh, ll, rest = scores(1, res, load)
    got = swap(far, "coeffici", CORE)
    near, nh, nl = scores(0, rest, lh, ll)
    own = own_block(near, got, *ring_swap([near[n] + got[n] for n in (1, 2, 3)], "coeffici", X))
    p1, p2, p3 = ring_swap([own] * 3, "coeffici", X)
    far_a = swap(jnp.stack([own, p1]), "coeffici", CORE)
    early = (stage(own, p1), nh, nl, stage(far_a), fh, fl)
    leave = covariance_pair((2, 3), 0, early, ())
    third = covariance_third(0, early)
    keep = covariance_pair((0, 1), 0, early, ())
    far_b = swap(jnp.stack([p2, p3]), "coeffici", CORE)
    near_b, other_b = (stage(p2, p3), nh, nl), (stage(far_b), fh, fl)
    leave = covariance_pair((2, 3), 1, near_b, leave)
    leave_p, leave_q = covariance_pair((2, 3), 1, other_b, leave)
    one_p = swap(leave_p, "particle", Y)
    one_q = swap(leave_q, "particle", 3 * Y)
    third = covariance_third(1, near_b + other_b, third)
    sums = ring_swap([third[4 * n : 4 * n + 4] for n in (1, 2, 3)], "particle", Z)
    keep_p, keep_q = covariance_pair((0, 1), 1, near_b + other_b, keep)
    two_p = swap(keep_p[4:] + one_p[4:], "particle", 3 * Y)
    two_q = swap(keep_q[4:] + one_q[4:], "particle", Y)

    def at_z(n):
        return jnp.concatenate([keep_p[n] + one_p[n] + two_p[n], keep_q[n] + one_q[n] + two_q[n]])

    def at_y(n):
        return third[n] + (sums[0][n] + sums[1][n]) + sums[2][n]

    r1, r2, r3 = ring_swap([at_z(n) for n in (1, 2, 3)], "particle", Z)
    t1, t2, t3 = ring_swap([at_y(n) for n in (1, 2, 3)], "particle", Y)
    mine = jnp.concatenate([at_z(0) + (r1 + r2) + r3, at_y(0) + (t1 + t2) + t3], axis=1)
    other = swap(mine, "half", 1)
    w, corr = shrink(factor, lh, ll, mine, other)

    corr = corr[0] + swap(corr[1], "coeffici", CORE)
    corr = ring_sum(corr, "coeffici", X)
    corr = ring_sum(corr, "particle", Z)
    far0 = swap(corr, "coeffici", CORE)
    got = ring_swap([jnp.stack([corr, w[n]]) for n in (1, 2, 3)], "particle", Y)
    far = swap(jnp.stack([g[0] for g in got]), "coeffici", CORE)
    weighted = place(w, *got)
    rayleigh = assemble(corr, *got, far0, far)
    return weighted[None], rayleigh[None]


def solution(mesh):
    in_specs = (P("half", "particle", "coeffici"), P("half", "coeffici", None))
    out_specs = (P("half", ("coeffici", "particle"), None), P("half", None, None))
    return jax.shard_map(step, mesh=mesh, in_specs=in_specs, out_specs=out_specs, check_vma=False)
```

```python
import functools

import jax
import jax.numpy as jnp
from jax import lax
from jax.experimental import pallas as pl
from jax.experimental.pallas import tpu as pltpu
from jax.sharding import PartitionSpec as P


F32 = jnp.float32
BF16 = jnp.bfloat16
VMEM = pl.BlockSpec(memory_space=pltpu.VMEM)
HBM = pl.BlockSpec(memory_space=pltpu.HBM)
LANE = 128

RING = (0, 1, 3, 2)
CORE, X, Y, Z = 1, 2, 4, 1
PLACES = ((0, 3, 1, 2), (0, 1, 3, 2))


def swap(value, axis, mask):
    return lax.ppermute(value, axis, [(s, s ^ mask) for s in range(lax.axis_size(axis))])


def split(value):
    high = value.astype(BF16)
    return high, (value - high.astype(F32)).astype(BF16)


def dot(left, right):
    return lax.dot_general(left, right, (((1,), (0,)), ((), ())), preferred_element_type=F32)


def dot3(lh, ll, rh, rl):
    return dot(lh, rh) + dot(ll, rh) + dot(lh, rl)


def at(index, size):
    return pl.ds(pl.multiple_of(index * size, size), size)


def params(mib):
    return pltpu.CompilerParams(vmem_limit_bytes=mib << 20)


def shape(*dims, dtype=F32):
    return jax.ShapeDtypeStruct(dims, dtype)


def cost(flops, mib):
    return pl.CostEstimate(flops=flops, bytes_accessed=mib << 20, transcendentals=0)


def scores_kernel(side, *refs):
    if side:
        res, load, out, rh, rl, lh, ll, later, rbuf, lbuf, acc, rsems, lsems, nsems = refs
    else:
        rbuf, lh, ll, out, rh, rl, acc = refs
    me = lax.axis_index("coeffici")
    size = out.shape[1]
    depth = lh.shape[0] // 4
    copies, others = [[] for _ in range(4)], []
    if side:
        for step in range(4):
            cols = slice(step * depth, (step + 1) * depth)
            copies[step].append(pltpu.make_async_copy(load.at[cols], lbuf.at[cols], lsems.at[step]))
            for t in range(4):
                copies[step].append(
                    pltpu.make_async_copy(
                        res.at[at(me ^ 1 ^ (X * RING[t]), size), cols], rbuf.at[pl.ds(t * size, size), cols], rsems.at[step, t]
                    )
                )
        for t in range(4):
            others.append(
                pltpu.make_async_copy(res.at[at(me ^ (X * RING[t]), size)], later.at[pl.ds(t * size, size)], nsems.at[t])
            )
        for copy in copies[0] + copies[1]:
            copy.start()
    for step in range(4):
        for copy in copies[step]:
            copy.wait()
        for copy in (copies[2], copies[3] + others[:1], others[1:], ())[step] if side else ():
            copy.start()
        cols = slice(step * depth, (step + 1) * depth)
        if side:
            lh[cols], ll[cols] = split(lbuf[cols])
        high, low = split(rbuf[:, cols])
        rh[:, cols], rl[:, cols] = high, low
        term = dot3(high, low, lh[cols], ll[cols])
        if step == 0:
            acc[...] = term
        else:
            acc[...] += term
    for t in range(4):
        out[t] = acc[t * size : (t + 1) * size]
    for copy in others:
        copy.wait()


def scores(side, res, *load):
    rows, coefs = res.shape
    rows = rows if side else 2 * rows
    k = load[0].shape[1]
    operand = shape(rows // 2, coefs, dtype=BF16)
    extra = (shape(coefs, k, dtype=BF16),) * 2 + (shape(rows // 2, coefs),)
    acc = pltpu.VMEM((rows // 2, k), F32)
    dma = pltpu.SemaphoreType.DMA
    return pl.pallas_call(
        functools.partial(scores_kernel, side),
        out_shape=(shape(4, rows // 8, k), operand, operand) + (extra if side else ()),
        in_specs=[HBM, HBM] if side else [VMEM] * 3,
        out_specs=(VMEM,) * (6 if side else 3),
        scratch_shapes=[pltpu.VMEM((rows // 2, coefs), F32), pltpu.VMEM((coefs, k), F32), acc, dma((4, 4)), dma((4,)), dma((4,))]
        if side
        else [acc],
        compiler_params=params(20),
        cost_estimate=cost(3 * rows * coefs * k, 6),
        name="scores_far" if side else "scores_near",
    )(res, *load)


def own_kernel(near, got, r1, r2, r3, out):
    out[...] = ((near[0] + got[0]) + (r1[...] + r2[...]) + r3[...]).T


def own_block(*terms):
    _, rows, k = terms[0].shape
    return pl.pallas_call(
        own_kernel,
        out_shape=shape(k, rows),
        in_specs=[VMEM] * 5,
        out_specs=VMEM,
        compiler_params=params(4),
        cost_estimate=cost(1 << 18, 1),
        name="own_block",
    )(*terms)


def stage_kernel(*refs):
    pieces, out = refs[:-1], refs[-1]
    for n in range(2):
        high, low = split(pieces[n][...] if len(pieces) == 2 else pieces[0][n])
        where = slice(n * LANE, (n + 1) * LANE)
        for block in range(4):
            rows = slice(64 * block, 64 * block + 64)
            out[128 * block : 128 * block + 64, where] = high[rows]
            out[128 * block + 64 : 128 * block + 128, where] = low[rows]


def stage(*pieces):
    return pl.pallas_call(
        stage_kernel,
        out_shape=shape(4 * LANE, 2 * LANE, dtype=BF16),
        in_specs=[VMEM] * len(pieces),
        out_specs=VMEM,
        compiler_params=params(4),
        cost_estimate=cost(1 << 18, 1),
        name="stage",
    )(*pieces)


def columns(refs, half, ys, zs):
    rows = slice(2 * LANE * half, 2 * LANE * (half + 1))
    return [jnp.concatenate([r[rows, at(4 * y + z, LANE)] for z in zs for y in ys], axis=1) for r in refs]


def pair_kernel(places, halves, sides, add, *refs):
    ops, before, (out_p, out_q) = refs[: 3 * sides], refs[3 * sides : 3 * sides + 2 * add], refs[-2:]
    particle = lax.axis_index("particle")
    y, z = particle >> 2, particle & 3
    starts = [(y ^ PLACES[part][place]) * LANE + 32 * part for part in range(2) for place in places]
    starts += [s + 64 for s in starts]
    wide = out_p.shape[2]

    @pl.loop(0, 2)
    def _(step):
        spots = [2 * step, 2 * step + 1]
        total = None
        for side in range(sides):
            st, rh, rl = ops[3 * side : 3 * side + 3]
            high, rest = columns((rh, rl), halves[side], range(3), [z ^ s ^ (s >> 1) for s in spots])
            left = jnp.concatenate([st[pl.ds(pl.multiple_of(s, 32), 32)] for s in starts])
            both, low = dot(left, high), dot(left[:LANE], rest)
            term = both[:LANE] + both[LANE:] + low
            total = term if total is None else total + term
        for part, out in enumerate((out_p, out_q)):
            for n in range(2):
                for i, spot in enumerate(spots):
                    top = 64 * part + 32 * n
                    value = total[top : top + 32, wide * i : wide * (i + 1)]
                    if add:
                        value = value + before[part][4 * n + spot]
                    out[4 * n + spot] = value


def covariance_pair(places, halves, operands, before):
    rows, coefs = operands[1].shape
    sides = len(operands) // 3
    out = shape(8, 32, 3 * LANE)
    return pl.pallas_call(
        functools.partial(pair_kernel, places, halves, sides, len(before) // 2),
        out_shape=(out, out),
        in_specs=[VMEM] * (len(operands) + len(before)),
        out_specs=(VMEM, VMEM),
        compiler_params=params(16),
        cost_estimate=cost(2 * rows * coefs * LANE * sides, 4),
    )(*operands, *before)


def third_kernel(half, *refs):
    ops, before, out = refs[:6], refs[6:-1], refs[-1]
    particle = lax.axis_index("particle")
    y, z = particle >> 2, particle & 3

    @pl.loop(0, 2)
    def _(step):
        spots = [2 * step, 2 * step + 1]
        both = low = None
        for st, rh, rl in (ops[:3], ops[3:]):
            high, rest = columns((rh, rl), half, [3], [z ^ s ^ (s >> 1) for s in spots])
            left_high = jnp.concatenate([st[LANE * b : LANE * b + 64] for b in range(4)])
            first, second = dot(st[...], high), dot(left_high, rest)
            both = first if both is None else both + first
            low = second if low is None else low + second
        for b in range(4):
            mask = y ^ b
            place = mask ^ (mask >> 1)
            top = LANE * b
            value = both[top : top + 64] + both[top + 64 : top + LANE] + low[64 * b : 64 * b + 64]
            for i, spot in enumerate(spots):
                mine = value[:, LANE * i : LANE * (i + 1)]
                out[4 * spot + place] = mine + before[0][4 * spot + place] if before else mine


def covariance_third(half, operands, *before):
    rows, coefs = operands[1].shape
    return pl.pallas_call(
        functools.partial(third_kernel, half),
        out_shape=shape(16, 64, LANE),
        in_specs=[VMEM] * (6 + len(before)),
        out_specs=VMEM,
        compiler_params=params(16),
        cost_estimate=cost(3 * rows * coefs * LANE, 4),
        name="covariance_third",
    )(*operands, *before)


def shrink_kernel(factor, load_h, load_l, mine, other, w_out, corr_out, cbuf):
    particle = lax.axis_index("particle")
    y, z = particle >> 2, particle & 3
    core = lax.axis_index("coeffici") & 1
    corr = None
    for n in range(4):
        cols = slice(n * LANE, n * LANE + LANE)
        cov = mine[:, cols] * factor
        far = other[:, cols] * factor
        weighted = cov * jax.nn.sigmoid(cov * far)
        mask = y ^ n
        w_out[mask ^ (mask >> 1)] = weighted
        wh, wl = split(weighted)
        where = at(4 * n + z, LANE)
        term = dot3(wh, wl, load_h[where], load_l[where])
        corr = term if corr is None else corr + term
    cbuf[...] = corr * factor
    for n in range(2):
        rows = cbuf[at(core ^ n, 32)]
        corr_out[n, :32] = rows[:, :LANE]
        corr_out[n, 32:] = rows[:, LANE:]


def shrink(factor, *args):
    return pl.pallas_call(
        functools.partial(shrink_kernel, factor),
        out_shape=(shape(4, 64, LANE), shape(2, 64, LANE)),
        in_specs=[VMEM] * 4,
        out_specs=(VMEM, VMEM),
        scratch_shapes=[pltpu.VMEM((64, 2 * LANE), F32)],
        compiler_params=params(8),
        cost_estimate=cost(6 * 64 * 512 * 256, 1),
        name="shrink",
    )(*args)


def place_kernel(w, r1, r2, r3, out, buf):
    y = lax.axis_index("particle") >> 2
    for mask, piece in zip(RING, (w[0], r1[1], r2[1], r3[1])):
        buf[at(y ^ mask, 64)] = piece
    out[...] = buf[...].T


def assemble_kernel(near0, r1, r2, r3, far0, far, out, buf):
    y = lax.axis_index("particle") >> 2
    core = lax.axis_index("coeffici") & 1
    near = (near0[...], r1[0], r2[0], r3[0])
    for n in range(4):
        for c, piece in enumerate((near[n], far0[...] if n == 0 else far[n - 1])):
            where = at(2 * (y ^ RING[n]) + (core ^ c), 32)
            buf[where, :LANE] = piece[:32]
            buf[where, LANE:] = piece[32:]
    out[...] = buf[...].T


def place(*args):
    return pl.pallas_call(
        place_kernel,
        out_shape=shape(LANE, 2 * LANE),
        in_specs=[VMEM] * len(args),
        out_specs=VMEM,
        scratch_shapes=[pltpu.VMEM((2 * LANE, LANE), F32)],
        compiler_params=params(4),
        cost_estimate=cost(1 << 18, 1),
        name="place",
    )(*args)


def assemble(*args):
    k = 2 * LANE
    return pl.pallas_call(
        assemble_kernel,
        out_shape=shape(k, k),
        in_specs=[VMEM] * len(args),
        out_specs=VMEM,
        scratch_shapes=[pltpu.VMEM((k, k), F32)],
        compiler_params=params(4),
        name="assemble",
    )(*args)


def ring_swap(values, axis, unit):
    swapped = []
    for v, m in zip(values, RING[1:]):
        swapped.append(swap(v, axis, unit * m))
    return swapped


def ring_sum(value, axis, unit):
    a, b, c = ring_swap([value] * 3, axis, unit)
    return (value + a) + (b + c)


def step(residuals, loadings):
    res, load = (pltpu.with_memory_space_constraint(v[0], pltpu.HBM) for v in (residuals, loadings))
    factor = (res.shape[0] * lax.axis_size("particle")) ** -0.5

    far, fh, fl, lh, ll, rest = scores(1, res, load)
    got = swap(far, "coeffici", CORE)
    near, nh, nl = scores(0, rest, lh, ll)
    own = own_block(near, got, *ring_swap([near[n] + got[n] for n in (1, 2, 3)], "coeffici", X))
    p1, p2, p3 = ring_swap([own] * 3, "coeffici", X)
    far_a = swap(jnp.stack([own, p1]), "coeffici", CORE)
    early = (stage(own, p1), nh, nl, stage(far_a), fh, fl)
    leave = covariance_pair((2, 3), (0, 0), early, ())
    third = covariance_third(0, early)
    far_b = swap(jnp.stack([p2, p3]), "coeffici", CORE)
    near_b, other_b = (stage(p2, p3), nh, nl), (stage(far_b), fh, fl)
    leave = covariance_pair((2, 3), (1,), near_b, leave)
    leave_p, leave_q = covariance_pair((2, 3), (1,), other_b, leave)
    one_p = swap(leave_p, "particle", Y)
    one_q = swap(leave_q, "particle", 3 * Y)
    third = covariance_third(1, near_b + other_b, third)
    sums = ring_swap([third[4 * n : 4 * n + 4] for n in (1, 2, 3)], "particle", Z)
    keep_p, keep_q = covariance_pair((0, 1), (0, 0, 1, 1), early + near_b + other_b, ())
    two_p = swap(keep_p[4:] + one_p[4:], "particle", 3 * Y)
    two_q = swap(keep_q[4:] + one_q[4:], "particle", Y)

    def at_z(n):
        return jnp.concatenate([keep_p[n] + one_p[n] + two_p[n], keep_q[n] + one_q[n] + two_q[n]])

    def at_y(n):
        return third[n] + (sums[0][n] + sums[1][n]) + sums[2][n]

    r1, r2, r3 = ring_swap([at_z(n) for n in (1, 2, 3)], "particle", Z)
    t1, t2, t3 = ring_swap([at_y(n) for n in (1, 2, 3)], "particle", Y)
    mine = jnp.concatenate([at_z(0) + (r1 + r2) + r3, at_y(0) + (t1 + t2) + t3], axis=1)
    other = swap(mine, "half", 1)
    w, corr = shrink(factor, lh, ll, mine, other)

    corr = corr[0] + swap(corr[1], "coeffici", CORE)
    corr = ring_sum(corr, "coeffici", X)
    corr = ring_sum(corr, "particle", Z)
    far0 = swap(corr, "coeffici", CORE)
    got = ring_swap([jnp.stack([corr, w[n]]) for n in (1, 2, 3)], "particle", Y)
    far = swap(jnp.stack([g[0] for g in got]), "coeffici", CORE)
    weighted = place(w, *got)
    rayleigh = assemble(corr, *got, far0, far)
    return weighted[None], rayleigh[None]


def solution(mesh):
    in_specs = (P("half", "particle", "coeffici"), P("half", "coeffici", None))
    out_specs = (P("half", ("coeffici", "particle"), None), P("half", None, None))
    return jax.shard_map(step, mesh=mesh, in_specs=in_specs, out_specs=out_specs, check_vma=False)
```
